256 devices in a mesh: dp: 128 (over x, y, z), head: 2 (over core).
Axes of the slice: x: 4, y: 4, z: 8, core: 2. Of those that a mesh axis runs over, the one named last changes fastest.
Arguments:
- context: bfloat16 [49152, 2048], P('dp', 'head'), may hold values from -6 to 6
- residual: bfloat16 [49152, 2048], P('dp'), may hold values from -6 to 6
- bias_out: float32 [2048], replicated, may hold values from -3 to 3
- norm_gain: float32 [2048], replicated, may hold values from 0.1 to 1.9
- out_weight: bfloat16 [2048, 2048], P('head', 'dp'), may hold values from -0.125 to 0.125
- cotangent: bfloat16 [49152, 2048], P('dp'), may hold values from -6 to 6
- counts: int32 [128], P('dp'), may hold values from 96 to 384, as said below
- slot_codes: int32 [49152], P('dp'), may hold values from 0 to 383, as said below
Outputs:
- grad_resid: bfloat16 [49152, 2048], P('dp')
- grad_ctx: bfloat16 [49152, 2048], P('dp', 'head')
- grad_wout: float32 [2048, 2048], P('head', 'dp')
The draws below stay inside these ranges and needn't reach their ends.
Inputs may be any that keep to these rules, and one draw needn't show every extreme that they name: `counts`: one dp index has 384 live rows, every other between 96 and 192. `slot_codes`: the codes of one device are distinct; code c names decoder owner c // 3 and slot c % 3; on every device the first 3 rows go to one owner.
All inputs are finite; a program needn't handle non-finite values.
Results may differ from the reference program's by a relative error of at most 0.0049.
Values may be sent and summed in bfloat16 or wider, within the bound.
No kernel may reach another device: no remote copies, remote signals or barrier semaphores. Data moves between devices by JAX's collectives and lax.ppermute only.
A program may use at most 64 MiB of HBM per device.

```python
import jax
import jax.numpy as jnp
from jax import lax

D = 2048
CAP = 384
REPLICAS = 128
SLOT = 3
BUFFER = 384
TOKENS = 49152
N_DP = 128


def draw_counts(key, part):
    key_low, key_top = jax.random.split(jax.random.fold_in(key, 11))
    lowered = jax.random.randint(key_low, (REPLICAS,), CAP // 4, CAP // 2 + 1)
    busiest = jax.random.randint(key_top, (), 0, REPLICAS)
    return jnp.where(jnp.arange(REPLICAS) == busiest, CAP, lowered).astype(jnp.int32)


def draw_slot_codes(key, part):
    base_key = jax.random.fold_in(key, 23)

    def per_device(device):
        device_key = jax.random.fold_in(base_key, device)
        key_order, key_rest = jax.random.split(device_key)
        order = jax.random.permutation(key_order, REPLICAS)
        code_seq = (order[:, None] * SLOT + jnp.arange(SLOT)[None, :]).reshape(-1)
        shuffled = jax.random.permutation(key_rest, code_seq[SLOT:])
        return jnp.concatenate([code_seq[:SLOT], shuffled])[:CAP]
    return jax.vmap(per_device)(jnp.arange(REPLICAS)).reshape(-1).astype(jnp.int32)


def levels(stream_key, shape, shards, low, largest):
    def one(axis_at, blocks):
        steps = jax.random.uniform(jax.random.fold_in(jax.random.fold_in(stream_key, 6), axis_at), (blocks,), jnp.float32, low / len(shards), largest / len(shards))
        return jnp.repeat(jnp.exp(steps), shape[axis_at] // blocks).reshape((-1,) + (1,) * (len(shape) - axis_at - 1))

    factor_of = one(*shards[0])
    for cut in shards[1:]:
        factor_of = factor_of * one(*cut)
    return factor_of


def bell_draw(key, extent, deviation, most, cuts=(), held_as=jnp.bfloat16):
    drawn = jax.random.normal(key, extent, jnp.float32) * deviation
    if len(cuts) > 0:
        drawn = levels(key, extent, cuts, -0.22, 0.18) * drawn
    return jnp.clip(drawn, min=-most, max=most).astype(held_as)


def setup_inputs(seed: int = 0) -> dict:
    key_of = jax.random.split(jax.random.key(seed), 9)
    context = bell_draw(key_of[0], (TOKENS, D), 1.0, 6.0, ((0, 128), (1, 2)))
    residual = bell_draw(key_of[1], (TOKENS, D), 1.0, 6.0, ((0, 128),))
    bias_out = bell_draw(key_of[2], (D,), 0.5, 3.0, (), jnp.float32)
    norm_gain = jnp.clip(1.0 + 0.18 * jax.random.normal(key_of[3], (D,), jnp.float32), 0.1, 1.9)
    out_weight = bell_draw(key_of[4], (D, D), D ** -0.5, 0.125, ((0, 2), (1, 128)))
    cotangent = bell_draw(key_of[5], (N_DP * BUFFER, D), 1.0, 6.0, ((0, 128),))
    counts = draw_counts(jax.random.fold_in(key_of[8], 71), 0)
    slot_codes = draw_slot_codes(jax.random.fold_in(key_of[8], 71), 0)
    return {"context": context, "residual": residual, "bias_out": bias_out, "norm_gain": norm_gain, "out_weight": out_weight, "cotangent": cotangent, "counts": counts, "slot_codes": slot_codes}


def reference(context, residual, bias_out, norm_gain, out_weight, cotangent, counts, slot_codes):
    row_ids = jnp.arange(REPLICAS * CAP, dtype=jnp.int32)
    device_of = row_ids // CAP
    position = row_ids % CAP
    live_mask = position < jnp.take(counts, device_of)
    owner_of = slot_codes // SLOT
    slot_of = slot_codes % SLOT
    row_index = (owner_of * BUFFER + device_of * SLOT + slot_of).astype(jnp.int32)
    picked = jnp.take(cotangent, row_index, axis=0)
    grad_out = jnp.where(live_mask[:, None], picked, jnp.zeros((), picked.dtype))
    projected = jnp.dot(context, out_weight, preferred_element_type=jnp.float32)
    summed_in = residual.astype(jnp.float32) + projected + bias_out
    mean_in = lax.optimization_barrier(jnp.mean(summed_in, axis=-1, keepdims=True))
    centred = summed_in - mean_in
    variance = lax.optimization_barrier(jnp.mean(centred * centred, axis=-1, keepdims=True))
    inv_std = lax.rsqrt(variance + 1e-05)
    normed = centred * inv_std
    grad_norm = grad_out.astype(jnp.float32) * norm_gain
    first_mean = lax.optimization_barrier(jnp.mean(grad_norm, axis=-1, keepdims=True))
    second_mean = lax.optimization_barrier(jnp.mean(grad_norm * normed, axis=-1, keepdims=True))
    grad_resid = (inv_std * (grad_norm - first_mean - normed * second_mean)).astype(jnp.bfloat16)
    grad_ctx = jnp.dot(grad_resid, out_weight.T, preferred_element_type=jnp.float32).astype(jnp.bfloat16)
    grad_wout = jnp.dot(context.T, grad_resid, preferred_element_type=jnp.float32) / REPLICAS
    return (grad_resid, grad_ctx, grad_wout)
```

```python
import jax
import jax.numpy as jnp
from jax import lax
from jax.sharding import Mesh, PartitionSpec as P

F32 = jnp.float32
BF16 = jnp.bfloat16


def norm_back(projected, residual, bias_out, norm_gain, grad_out):
    summed_in = residual.astype(F32) + projected + bias_out
    mean_in = jnp.mean(summed_in, axis=-1, keepdims=True)
    centred = summed_in - mean_in
    variance = jnp.mean(centred * centred, axis=-1, keepdims=True)
    inv_std = lax.rsqrt(variance + 1e-05)
    normed = centred * inv_std
    grad_norm = grad_out.astype(F32) * norm_gain
    first_mean = jnp.mean(grad_norm, axis=-1, keepdims=True)
    second_mean = jnp.mean(grad_norm * normed, axis=-1, keepdims=True)
    return (inv_std * (grad_norm - first_mean - normed * second_mean)).astype(BF16)


def shards(context, residual, bias_out, norm_gain, out_weight, cotangent, counts, slot_codes):
    capacity = slot_codes.shape[0]
    features = residual.shape[1]
    half = features // 2
    core = lax.axis_index("core")
    live_mask = jnp.arange(capacity) < counts[0]
    swap = [(0, 1), (1, 0)]

    mine = lax.dynamic_slice_in_dim(cotangent, core * half, half, axis=1)
    returned = lax.all_to_all(mine, ("x", "y", "z"), split_axis=0, concat_axis=0, tiled=True)
    picked = jnp.take(returned, slot_codes, axis=0)
    picked = jnp.where(live_mask[:, None], picked, jnp.zeros((), picked.dtype))
    other = lax.ppermute(picked, "core", swap)
    grad_out = jnp.where(
        core == 0,
        jnp.concatenate([picked, other], axis=1),
        jnp.concatenate([other, picked], axis=1),
    )

    weight_t = lax.all_gather(out_weight.T, "z", axis=0, tiled=True)
    weight_t = lax.all_gather(weight_t, ("x", "y"), axis=0, tiled=True)

    partial_proj = lax.dot_general(
        context, weight_t, (((1,), (1,)), ((), ())), preferred_element_type=F32
    )
    projected = partial_proj + lax.ppermute(partial_proj, "core", swap)
    grad_resid = norm_back(projected, residual, bias_out, norm_gain, grad_out)

    share = lax.dot_general(
        grad_resid, context, (((0,), (0,)), ((), ())), preferred_element_type=F32
    ).astype(BF16)
    grad_ctx = jnp.dot(grad_resid, weight_t, preferred_element_type=F32).astype(BF16)
    total = None
    for axis in ("x", "y", "z"):
        ways = lax.axis_size(axis)
        share = share.reshape(ways, -1, share.shape[-1])
        got = lax.all_to_all(share, axis, split_axis=0, concat_axis=0)
        total = jnp.sum(got.astype(F32), axis=0)
        share = total.astype(BF16)
    replicas = lax.axis_size("x") * lax.axis_size("y") * lax.axis_size("z")
    grad_wout = (total / replicas).T
    return (grad_resid, grad_ctx, grad_wout)


def solution(mesh):
    torus = Mesh(mesh.devices.reshape(4, 4, 8, 2), ("x", "y", "z", "core"))
    dp = ("x", "y", "z")
    return jax.shard_map(
        shards,
        mesh=torus,
        in_specs=(
            P(dp, "core"),
            P(dp, None),
            P(),
            P(),
            P("core", dp),
            P(dp, None),
            P(dp),
            P(dp),
        ),
        out_specs=(P(dp, None), P(dp, "core"), P("core", dp)),
        check_vma=False,
    )
```

```python
import functools

import jax
import jax.numpy as jnp
from jax import lax
from jax.experimental import pallas as pl
from jax.experimental.pallas import tpu as pltpu
from jax.sharding import Mesh, PartitionSpec as P

F32 = jnp.float32
BF16 = jnp.bfloat16
RIGHT = [(i, (i + 1) % 4) for i in range(4)]
LEFT = [(i, (i - 1) % 4) for i in range(4)]


def norm_back(projected, residual, bias_out, norm_gain, grad_out):
    summed_in = residual.astype(F32) + projected + bias_out
    mean_in = jnp.mean(summed_in, axis=-1, keepdims=True)
    centred = summed_in - mean_in
    variance = jnp.mean(centred * centred, axis=-1, keepdims=True)
    inv_std = lax.rsqrt(variance + 1e-05)
    normed = centred * inv_std
    grad_norm = grad_out.astype(F32) * norm_gain
    first_mean = jnp.mean(grad_norm, axis=-1, keepdims=True)
    second_mean = jnp.mean(grad_norm * normed, axis=-1, keepdims=True)
    return (inv_std * (grad_norm - first_mean - normed * second_mean)).astype(BF16)


def ring_gather(piece, axis):
    mid = piece.shape[0] // 2
    before = lax.ppermute(piece, axis, RIGHT)
    after = lax.ppermute(piece, axis, LEFT)
    top = lax.ppermute(before[:mid], axis, RIGHT)
    bottom = lax.ppermute(after[mid:], axis, LEFT)
    return piece, after, top, bottom, before


def ring_reduce(chunk_of, axis):
    far = chunk_of(2).astype(BF16)
    mid = far.shape[0] // 2
    top = lax.ppermute(far[:mid], axis, RIGHT)
    bottom = lax.ppermute(far[mid:], axis, LEFT)
    ahead, behind = chunk_of(1), chunk_of(3)
    ahead = jnp.concatenate([ahead[:mid] + top.astype(F32), ahead[mid:]]).astype(BF16)
    behind = jnp.concatenate([behind[:mid], behind[mid:] + bottom.astype(F32)]).astype(BF16)
    from_before = lax.ppermute(ahead, axis, RIGHT)
    from_after = lax.ppermute(behind, axis, LEFT)
    return chunk_of(0) + from_before.astype(F32) + from_after.astype(F32)


def place_kernel(*refs):
    a_refs, b_refs, out_ref, sems = refs[:5], refs[5:10], refs[10], refs[11]
    ix, iy = lax.axis_index("x"), lax.axis_index("y")
    copies = []
    k = 0
    for ref, step, low in zip(a_refs, (0, 1, 2, 2, 3), (0, 0, 0, 2, 0)):
        at = lax.rem(ix + step, 4)
        size = ref.shape[0]
        copies.append(pltpu.make_async_copy(
            ref, out_ref.at[at, pl.ds(low, size), :, pl.ds(0, 512)], sems.at[k]))
        k += 1
    for ref, step, low in zip(b_refs, (0, 1, 2, 2, 3), (0, 0, 0, 2, 0)):
        at = lax.rem(iy + step, 4)
        size = ref.shape[0]
        copies.append(pltpu.make_async_copy(
            ref, out_ref.at[pl.ds(low, size), at, :, pl.ds(512, 512)], sems.at[k]))
        k += 1
    for copy in copies:
        copy.start()
    for copy in copies:
        copy.wait()


def place_weight(a_pieces, b_pieces):
    return pl.pallas_call(
        place_kernel,
        out_shape=jax.ShapeDtypeStruct((4, 4, 128, 1024), BF16),
        in_specs=[pl.BlockSpec(memory_space=pl.ANY)] * 10,
        out_specs=pl.BlockSpec(memory_space=pl.ANY),
        scratch_shapes=[pltpu.SemaphoreType.DMA((10,))],
        cost_estimate=pl.CostEstimate(flops=0, bytes_accessed=8 << 20, transcendentals=0),
        name="place_weight",
    )(*a_pieces, *b_pieces)


def in_order(pieces, index):
    mine, after, top, bottom, before = pieces
    size = mine.shape[0]
    out = jnp.zeros((4,) + mine.shape, mine.dtype)
    def put(out, piece, step, low):
        at = lax.rem(index + step, 4)
        return lax.dynamic_update_slice(out, piece[None], (at, low, 0))
    out = put(out, mine, 0, 0)
    out = put(out, after, 1, 0)
    out = put(out, top, 2, 0)
    out = put(out, bottom, 2, size // 2)
    return put(out, before, 3, 0)


def gather_weight(weight_t, ix, iy):
    spread = jnp.broadcast_to(weight_t[None], (8,) + weight_t.shape)
    column = lax.all_to_all(spread, "z", split_axis=0, concat_axis=0)
    column = column.reshape(128, 1024)
    a = in_order(ring_gather(column[:, :512], "y"), iy)
    b = in_order(ring_gather(column[:, 512:], "x"), ix)
    a_pieces = ring_gather(a, "x")
    b_pieces = ring_gather(b, "y")
    return place_weight(a_pieces, b_pieces).reshape(2048, 1024)


def shards(context, residual, bias_out, norm_gain, out_weight, cotangent, counts, slot_codes):
    capacity = slot_codes.shape[0]
    features = residual.shape[1]
    half = features // 2
    core = lax.axis_index("core")
    ix, iy = lax.axis_index("x"), lax.axis_index("y")
    live_mask = jnp.arange(capacity) < counts[0]
    swap = [(0, 1), (1, 0)]

    mine = lax.dynamic_slice_in_dim(cotangent, core * half, half, axis=1)
    returned = lax.all_to_all(mine, ("x", "y", "z"), split_axis=0, concat_axis=0, tiled=True)
    picked = jnp.take(returned, slot_codes, axis=0)
    picked = jnp.where(live_mask[:, None], picked, jnp.zeros((), picked.dtype))
    other = lax.ppermute(picked, "core", swap)
    grad_out = jnp.where(
        core == 0,
        jnp.concatenate([picked, other], axis=1),
        jnp.concatenate([other, picked], axis=1),
    )

    weight_t = gather_weight(out_weight.T, ix, iy)

    partial_proj = lax.dot_general(
        context, weight_t, (((1,), (1,)), ((), ())), preferred_element_type=F32
    )
    projected = partial_proj + lax.ppermute(partial_proj, "core", swap)
    grad_resid = norm_back(projected, residual, bias_out, norm_gain, grad_out)

    def product(columns, left):
        return lax.dot_general(
            columns, left, (((0,), (0,)), ((), ())), preferred_element_type=F32
        )

    def a_chunk(step):
        at = lax.rem(ix + step, 4)
        return product(lax.dynamic_slice_in_dim(grad_resid, at * 512, 512, axis=1), context[:, :512])

    def b_chunk(step):
        at = lax.rem(iy + step, 4)
        strips = [
            lax.dynamic_slice_in_dim(grad_resid, (x * 4 + at) * 128, 128, axis=1) for x in range(4)
        ]
        return product(jnp.concatenate(strips, axis=1), context[:, 512:])

    a_sum = ring_reduce(a_chunk, "x")
    b_sum = ring_reduce(b_chunk, "y")

    def strip_of(total, index):
        return lambda step: lax.dynamic_slice_in_dim(total, lax.rem(index + step, 4) * 128, 128, axis=0)

    a_sum = ring_reduce(strip_of(a_sum, iy), "y")
    b_sum = ring_reduce(strip_of(b_sum, ix), "x")
    share = jnp.concatenate([a_sum, b_sum], axis=1).astype(BF16).reshape(8, 16, 1024)
    got = lax.all_to_all(share, "z", split_axis=0, concat_axis=0)
    total = jnp.sum(got.astype(F32), axis=0)
    replicas = lax.axis_size("x") * lax.axis_size("y") * lax.axis_size("z")
    grad_wout = (total / replicas).T
    grad_ctx = jnp.dot(grad_resid, weight_t, preferred_element_type=F32).astype(BF16)
    return (grad_resid, grad_ctx, grad_wout)


def solution(mesh):
    torus = Mesh(mesh.devices.reshape(4, 4, 8, 2), ("x", "y", "z", "core"))
    dp = ("x", "y", "z")
    return jax.shard_map(
        shards,
        mesh=torus,
        in_specs=(
            P(dp, "core"),
            P(dp, None),
            P(),
            P(),
            P("core", dp),
            P(dp, None),
            P(dp),
            P(dp),
        ),
        out_specs=(P(dp, None), P(dp, "core"), P("core", dp)),
        check_vma=False,
    )
```

```python
import jax
import jax.numpy as jnp
from jax import lax
from jax.experimental import pallas as pl
from jax.experimental.pallas import tpu as pltpu
from jax.sharding import Mesh, PartitionSpec as P

F32 = jnp.float32
BF16 = jnp.bfloat16
RIGHT = [(i, (i + 1) % 4) for i in range(4)]
LEFT = [(i, (i - 1) % 4) for i in range(4)]


def norm_back(projected, residual, bias_out, norm_gain, grad_out):
    summed_in = residual.astype(F32) + projected + bias_out
    mean_in = jnp.mean(summed_in, axis=-1, keepdims=True)
    centred = summed_in - mean_in
    variance = jnp.mean(centred * centred, axis=-1, keepdims=True)
    inv_std = lax.rsqrt(variance + 1e-05)
    normed = centred * inv_std
    grad_norm = grad_out.astype(F32) * norm_gain
    first_mean = jnp.mean(grad_norm, axis=-1, keepdims=True)
    second_mean = jnp.mean(grad_norm * normed, axis=-1, keepdims=True)
    return (inv_std * (grad_norm - first_mean - normed * second_mean)).astype(BF16)


def ring_gather(piece, axis):
    mid = piece.shape[0] // 2
    before = lax.ppermute(piece, axis, RIGHT)
    after = lax.ppermute(piece, axis, LEFT)
    top = lax.ppermute(before[:mid], axis, RIGHT)
    bottom = lax.ppermute(after[mid:], axis, LEFT)
    return piece, after, top, bottom, before


def ring_reduce(chunk_of, axis):
    far = chunk_of(2).astype(BF16)
    mid = far.shape[0] // 2
    top = lax.ppermute(far[:mid], axis, RIGHT)
    bottom = lax.ppermute(far[mid:], axis, LEFT)
    ahead, behind = chunk_of(1), chunk_of(3)
    ahead = jnp.concatenate([ahead[:mid] + top.astype(F32), ahead[mid:]]).astype(BF16)
    behind = jnp.concatenate([behind[:mid], behind[mid:] + bottom.astype(F32)]).astype(BF16)
    from_before = lax.ppermute(ahead, axis, RIGHT)
    from_after = lax.ppermute(behind, axis, LEFT)
    return chunk_of(0) + from_before.astype(F32) + from_after.astype(F32)


def project_kernel(*refs):
    context_ref, a_refs, b_refs = refs[0], refs[1:6], refs[6:11]
    weight_ref, out_ref = refs[11], refs[12]
    ix, iy = lax.axis_index("x"), lax.axis_index("y")
    steps, lows = (0, 1, 2, 2, 3), (0, 0, 0, 2, 0)
    for ref, step, low in zip(a_refs, steps, lows):
        at = lax.rem(ix + step, 4)
        weight_ref[at, low:low + ref.shape[0], :, 0:512] = ref[...]
    for ref, step, low in zip(b_refs, steps, lows):
        at = lax.rem(iy + step, 4)
        for k in range(ref.shape[0]):
            weight_ref[low + k, at, :, 512:1024] = ref[k]
    for x in range(4):
        block = weight_ref[x].reshape(512, 1024)
        out_ref[:, x * 512:(x + 1) * 512] = lax.dot_general(
            context_ref[...], block, (((1,), (1,)), ((), ())), preferred_element_type=F32
        )


def project(context, a_pieces, b_pieces):
    rows = context.shape[0]
    return pl.pallas_call(
        project_kernel,
        out_shape=(
            jax.ShapeDtypeStruct((4, 4, 128, 1024), BF16),
            jax.ShapeDtypeStruct((rows, 2048), F32),
        ),
        compiler_params=pltpu.CompilerParams(vmem_limit_bytes=40 << 20),
        cost_estimate=pl.CostEstimate(
            flops=2 * rows * 1024 * 2048, bytes_accessed=16 << 20, transcendentals=0
        ),
        name="project",
    )(context, *a_pieces, *b_pieces)


def spread(piece, axes):
    return lax.all_to_all(
        jnp.broadcast_to(piece[None], (32,) + piece.shape), axes, split_axis=0, concat_axis=0
    )


def collect(total, axes):
    share = total.astype(BF16).reshape(32, 16, 512)
    got = lax.all_to_all(share, axes, split_axis=0, concat_axis=0)
    return jnp.sum(got.astype(F32), axis=0)


def shards(context, residual, bias_out, norm_gain, out_weight, cotangent, counts, slot_codes):
    capacity = slot_codes.shape[0]
    features = residual.shape[1]
    half = features // 2
    core = lax.axis_index("core")
    ix, iy = lax.axis_index("x"), lax.axis_index("y")
    live_mask = jnp.arange(capacity) < counts[0]
    swap = [(0, 1), (1, 0)]

    mine = lax.dynamic_slice_in_dim(cotangent, core * half, half, axis=1)
    weight_t = out_weight.T
    mine, weight_t = lax.optimization_barrier((mine, weight_t))
    returned = lax.all_to_all(mine, ("x", "y", "z"), split_axis=0, concat_axis=0, tiled=True)
    a_block = spread(weight_t[:, :512], ("y", "z")).reshape(4, 128, 512)
    b_block = spread(weight_t[:, 512:], ("x", "z")).reshape(4, 128, 512)
    a_pieces = ring_gather(a_block, "x")
    b_pieces = ring_gather(b_block, "y")
    a_pieces, b_pieces, returned = lax.optimization_barrier((a_pieces, b_pieces, returned))

    weight_t, partial_proj = project(context, a_pieces, b_pieces)
    weight_t = weight_t.reshape(2048, 1024)
    picked = returned.at[slot_codes].get(mode="promise_in_bounds")
    picked = jnp.where(live_mask[:, None], picked, jnp.zeros((), picked.dtype))
    other = lax.ppermute(picked, "core", swap)
    grad_out = jnp.where(
        core == 0,
        jnp.concatenate([picked, other], axis=1),
        jnp.concatenate([other, picked], axis=1),
    )
    projected = partial_proj + lax.ppermute(partial_proj, "core", swap)
    grad_resid = norm_back(projected, residual, bias_out, norm_gain, grad_out)

    def product(columns, left):
        return lax.dot_general(
            columns, left, (((0,), (0,)), ((), ())), preferred_element_type=F32
        )

    def a_chunk(step):
        at = lax.rem(ix + step, 4)
        return product(lax.dynamic_slice_in_dim(grad_resid, at * 512, 512, axis=1), context[:, :512])

    def b_chunk(step):
        at = lax.rem(iy + step, 4)
        strips = [
            lax.dynamic_slice_in_dim(grad_resid, (x * 4 + at) * 128, 128, axis=1) for x in range(4)
        ]
        return product(jnp.concatenate(strips, axis=1), context[:, 512:])

    a_sum = ring_reduce(a_chunk, "x")
    b_sum = ring_reduce(b_chunk, "y")

    total = jnp.concatenate(
        [collect(a_sum, ("y", "z")), collect(b_sum, ("x", "z"))], axis=1
    )
    replicas = lax.axis_size("x") * lax.axis_size("y") * lax.axis_size("z")
    grad_wout = (total / replicas).T
    grad_ctx = jnp.dot(grad_resid, weight_t, preferred_element_type=F32).astype(BF16)
    return (grad_resid, grad_ctx, grad_wout)


def solution(mesh):
    torus = Mesh(mesh.devices.reshape(4, 4, 8, 2), ("x", "y", "z", "core"))
    dp = ("x", "y", "z")
    return jax.shard_map(
        shards,
        mesh=torus,
        in_specs=(
            P(dp, "core"),
            P(dp, None),
            P(),
            P(),
            P("core", dp),
            P(dp, None),
            P(dp),
            P(dp),
        ),
        out_specs=(P(dp, None), P(dp, "core"), P("core", dp)),
        check_vma=False,
    )
```

```python
import jax
import jax.numpy as jnp
from jax import lax
from jax.experimental import pallas as pl
from jax.experimental.pallas import tpu as pltpu
from jax.sharding import Mesh, PartitionSpec as P

F32 = jnp.float32
BF16 = jnp.bfloat16
RIGHT = [(i, (i + 1) % 4) for i in range(4)]
LEFT = [(i, (i - 1) % 4) for i in range(4)]


def norm_back(projected, residual, bias_out, norm_gain, grad_out):
    summed_in = residual.astype(F32) + projected + bias_out
    mean_in = jnp.mean(summed_in, axis=-1, keepdims=True)
    centred = summed_in - mean_in
    variance = jnp.mean(centred * centred, axis=-1, keepdims=True)
    inv_std = lax.rsqrt(variance + 1e-05)
    normed = centred * inv_std
    grad_norm = grad_out.astype(F32) * norm_gain
    first_mean = jnp.mean(grad_norm, axis=-1, keepdims=True)
    second_mean = jnp.mean(grad_norm * normed, axis=-1, keepdims=True)
    return (inv_std * (grad_norm - first_mean - normed * second_mean)).astype(BF16)


def ring_gather(piece, axis):
    mid = piece.shape[0] // 2
    before = lax.ppermute(piece, axis, RIGHT)
    after = lax.ppermute(piece, axis, LEFT)
    top = lax.ppermute(before[:mid], axis, RIGHT)
    bottom = lax.ppermute(after[mid:], axis, LEFT)
    return piece, after, top, bottom, before


def ring_columns(columns_of, axis):
    far = columns_of(2)
    rows = far.shape[0]
    mid = rows // 2
    right = jnp.concatenate([columns_of(1), far[:mid]])
    left = jnp.concatenate([columns_of(3), far[mid:]])
    before = lax.ppermute(right, axis, RIGHT)
    after = lax.ppermute(left, axis, LEFT)
    top = lax.ppermute(before[rows:], axis, RIGHT)
    bottom = lax.ppermute(after[rows:], axis, LEFT)
    return columns_of(0), after[:rows], top, bottom, before[:rows]


def project_kernel(*refs):
    context_ref, pieces = refs[0], refs[1:6]
    weight_ref, out_ref = refs[6], refs[7]
    iy = lax.axis_index("y")
    for ref, step, low in zip(pieces, (0, 1, 2, 2, 3), (0, 0, 0, 2, 0)):
        at = lax.rem(iy + step, 4)
        for k in range(ref.shape[0]):
            weight_ref[low + k, at] = ref[k]
    for x in range(4):
        block = weight_ref[x].reshape(512, 1024)
        out_ref[:, x * 512:(x + 1) * 512] = lax.dot_general(
            context_ref[...], block, (((1,), (1,)), ((), ())), preferred_element_type=F32
        )


def project(context, pieces):
    rows = context.shape[0]
    return pl.pallas_call(
        project_kernel,
        out_shape=(
            jax.ShapeDtypeStruct((4, 4, 128, 1024), BF16),
            jax.ShapeDtypeStruct((rows, 2048), F32),
        ),
        compiler_params=pltpu.CompilerParams(vmem_limit_bytes=40 << 20),
        cost_estimate=pl.CostEstimate(
            flops=2 * rows * 1024 * 2048, bytes_accessed=16 << 20, transcendentals=0
        ),
        name="project",
    )(context, *pieces)


def spread(piece, axes):
    return lax.all_to_all(
        jnp.broadcast_to(piece[None], (32,) + piece.shape), axes, split_axis=0, concat_axis=0
    )


def collect(total, axes):
    share = total.astype(BF16).reshape(32, 16, 1024)
    got = lax.all_to_all(share, axes, split_axis=0, concat_axis=0)
    return jnp.sum(got.astype(F32), axis=0)


def shards(context, residual, bias_out, norm_gain, out_weight, cotangent, counts, slot_codes):
    capacity = slot_codes.shape[0]
    features = residual.shape[1]
    half = features // 2
    core = lax.axis_index("core")
    ix = lax.axis_index("x")
    live_mask = jnp.arange(capacity) < counts[0]
    swap = [(0, 1), (1, 0)]

    mine = lax.dynamic_slice_in_dim(cotangent, core * half, half, axis=1)
    weight_t = out_weight.T
    mine, weight_t = lax.optimization_barrier((mine, weight_t))
    returned = lax.all_to_all(mine, ("x", "y", "z"), split_axis=0, concat_axis=0, tiled=True)
    block = spread(weight_t, ("x", "z")).reshape(4, 128, 1024)
    block, held = lax.optimization_barrier((block, context))
    context_pieces = ring_gather(held, "x")
    pieces = ring_gather(block, "y")
    pieces, returned = lax.optimization_barrier((pieces, returned))

    weight_t, partial_proj = project(context, pieces)
    weight_t = weight_t.reshape(2048, 1024)
    picked = returned.at[slot_codes].get(mode="promise_in_bounds")
    picked = jnp.where(live_mask[:, None], picked, jnp.zeros((), picked.dtype))
    other = lax.ppermute(picked, "core", swap)
    grad_out = jnp.where(
        core == 0,
        jnp.concatenate([picked, other], axis=1),
        jnp.concatenate([other, picked], axis=1),
    )
    projected = partial_proj + lax.ppermute(partial_proj, "core", swap)
    grad_resid = norm_back(projected, residual, bias_out, norm_gain, grad_out)

    def columns_of(step):
        at = lax.rem(ix + step, 4)
        return lax.dynamic_slice_in_dim(grad_resid, at * 512, 512, axis=1)

    share = jnp.zeros((), F32)
    for columns, rows in zip(ring_columns(columns_of, "x"), context_pieces):
        share = share + lax.dot_general(
            columns, rows, (((0,), (0,)), ((), ())), preferred_element_type=F32
        )
    total = collect(share, ("y", "z"))
    replicas = lax.axis_size("x") * lax.axis_size("y") * lax.axis_size("z")
    grad_wout = (total / replicas).T
    grad_ctx = jnp.dot(grad_resid, weight_t, preferred_element_type=F32).astype(BF16)
    return (grad_resid, grad_ctx, grad_wout)


def solution(mesh):
    torus = Mesh(mesh.devices.reshape(4, 4, 8, 2), ("x", "y", "z", "core"))
    dp = ("x", "y", "z")
    return jax.shard_map(
        shards,
        mesh=torus,
        in_specs=(
            P(dp, "core"),
            P(dp, None),
            P(),
            P(),
            P("core", dp),
            P(dp, None),
            P(dp),
            P(dp),
        ),
        out_specs=(P(dp, None), P(dp, "core"), P("core", dp)),
        check_vma=False,
    )
```

```python
import jax
import jax.numpy as jnp
from jax import lax
from jax.experimental import pallas as pl
from jax.experimental.pallas import tpu as pltpu
from jax.sharding import Mesh, PartitionSpec as P

F32 = jnp.float32
BF16 = jnp.bfloat16
RIGHT = [(i, (i + 1) % 4) for i in range(4)]
LEFT = [(i, (i - 1) % 4) for i in range(4)]


def norm_back(projected, residual, bias_out, norm_gain, grad_out):
    summed_in = residual.astype(F32) + projected + bias_out
    mean_in = jnp.mean(summed_in, axis=-1, keepdims=True)
    centred = summed_in - mean_in
    variance = jnp.mean(centred * centred, axis=-1, keepdims=True)
    inv_std = lax.rsqrt(variance + 1e-05)
    normed = centred * inv_std
    grad_norm = grad_out.astype(F32) * norm_gain
    first_mean = jnp.mean(grad_norm, axis=-1, keepdims=True)
    second_mean = jnp.mean(grad_norm * normed, axis=-1, keepdims=True)
    return (inv_std * (grad_norm - first_mean - normed * second_mean)).astype(BF16)


def ring_gather(piece, axis):
    mid = piece.shape[0] // 2
    before = lax.ppermute(piece, axis, RIGHT)
    after = lax.ppermute(piece, axis, LEFT)
    top = lax.ppermute(before[:mid], axis, RIGHT)
    bottom = lax.ppermute(after[mid:], axis, LEFT)
    return piece, after, top, bottom, before


def ring_reduce(chunk_of, axis):
    far = chunk_of(2).astype(BF16)
    mid = far.shape[0] // 2
    top = lax.ppermute(far[:mid], axis, RIGHT)
    bottom = lax.ppermute(far[mid:], axis, LEFT)
    ahead, behind = chunk_of(1), chunk_of(3)
    ahead = jnp.concatenate([ahead[:mid] + top.astype(F32), ahead[mid:]]).astype(BF16)
    behind = jnp.concatenate([behind[:mid], behind[mid:] + bottom.astype(F32)]).astype(BF16)
    from_before = lax.ppermute(ahead, axis, RIGHT)
    from_after = lax.ppermute(behind, axis, LEFT)
    return chunk_of(0) + from_before.astype(F32) + from_after.astype(F32)


def ring_columns(columns_of, axis):
    far = columns_of(2)
    rows = far.shape[0]
    mid = rows // 2
    right = jnp.concatenate([columns_of(1), far[:mid]])
    left = jnp.concatenate([columns_of(3), far[mid:]])
    before = lax.ppermute(right, axis, RIGHT)
    after = lax.ppermute(left, axis, LEFT)
    top = lax.ppermute(before[rows:], axis, RIGHT)
    bottom = lax.ppermute(after[rows:], axis, LEFT)
    return columns_of(0), after[:rows], top, bottom, before[:rows]


def project_kernel(*refs):
    context_ref, pieces = refs[0], refs[1:6]
    weight_ref, out_ref = refs[6], refs[7]
    ix, iy = lax.axis_index("x"), lax.axis_index("y")
    for ref, step, low in zip(pieces, (0, 1, 2, 2, 3), (0, 0, 0, 2, 0)):
        at = lax.rem(iy + step, 4)
        for k in range(ref.shape[0]):
            weight_ref[lax.rem(ix + low + k, 4), at] = ref[k]
    for x in range(4):
        block = weight_ref[x].reshape(512, 1024)
        out_ref[:, x * 512:(x + 1) * 512] = lax.dot_general(
            context_ref[...], block, (((1,), (1,)), ((), ())), preferred_element_type=F32
        )


def project(context, pieces):
    rows = context.shape[0]
    return pl.pallas_call(
        project_kernel,
        out_shape=(
            jax.ShapeDtypeStruct((4, 4, 128, 1024), BF16),
            jax.ShapeDtypeStruct((rows, 2048), F32),
        ),
        compiler_params=pltpu.CompilerParams(vmem_limit_bytes=40 << 20),
        cost_estimate=pl.CostEstimate(
            flops=2 * rows * 1024 * 2048, bytes_accessed=16 << 20, transcendentals=0
        ),
        name="project",
    )(context, *pieces)


def spread(piece, axis):
    ways = lax.axis_size(axis)
    whole = jnp.broadcast_to(piece[None], (ways,) + piece.shape)
    return lax.all_to_all(whole, axis, split_axis=0, concat_axis=0)


def collect(total, axis):
    ways = lax.axis_size(axis)
    share = total.astype(BF16).reshape(ways, -1, total.shape[1])
    got = lax.all_to_all(share, axis, split_axis=0, concat_axis=0)
    return jnp.sum(got.astype(F32), axis=0)


def shards(context, residual, bias_out, norm_gain, out_weight, cotangent, counts, slot_codes):
    capacity = slot_codes.shape[0]
    features = residual.shape[1]
    half = features // 2
    core = lax.axis_index("core")
    ix, iy = lax.axis_index("x"), lax.axis_index("y")
    live_mask = jnp.arange(capacity) < counts[0]
    swap = [(0, 1), (1, 0)]

    mine = lax.dynamic_slice_in_dim(cotangent, core * half, half, axis=1)
    weight_t = out_weight.T
    mine, weight_t = lax.optimization_barrier((mine, weight_t))
    returned = lax.all_to_all(mine, ("x", "y", "z"), split_axis=0, concat_axis=0, tiled=True)
    block = spread(weight_t, "z").reshape(128, 1024)
    context_before = lax.ppermute(context, "x", RIGHT)
    context_after = lax.ppermute(context, "x", LEFT)
    block, context_before, context_after = lax.optimization_barrier(
        (block, context_before, context_after)
    )
    mid = capacity // 2
    context_top = lax.ppermute(context_before[:mid], "x", RIGHT)
    context_bottom = lax.ppermute(context_after[mid:], "x", LEFT)
    context_pieces = (context, context_after, context_top, context_bottom, context_before)
    block = jnp.concatenate(ring_gather(block, "x")).reshape(4, 128, 1024)
    pieces = ring_gather(block, "y")
    pieces, returned, context_pieces = lax.optimization_barrier((pieces, returned, context_pieces))

    weight_t, partial_proj = project(context, pieces)
    weight_t = weight_t.reshape(2048, 1024)
    picked = returned.at[slot_codes].get(mode="promise_in_bounds")
    picked = jnp.where(live_mask[:, None], picked, jnp.zeros((), picked.dtype))
    other = lax.ppermute(picked, "core", swap)
    grad_out = jnp.where(
        core == 0,
        jnp.concatenate([picked, other], axis=1),
        jnp.concatenate([other, picked], axis=1),
    )
    projected = partial_proj + lax.ppermute(partial_proj, "core", swap)
    grad_resid = norm_back(projected, residual, bias_out, norm_gain, grad_out)

    def columns_of(step):
        at = lax.rem(ix + step, 4)
        return lax.dynamic_slice_in_dim(grad_resid, at * 512, 512, axis=1)

    share = jnp.zeros((), F32)
    for columns, rows in zip(ring_columns(columns_of, "x"), context_pieces):
        share = share + lax.dot_general(
            columns, rows, (((0,), (0,)), ((), ())), preferred_element_type=F32
        )
    def strip_of(step):
        return lax.dynamic_slice_in_dim(share, lax.rem(iy + step, 4) * 128, 128, axis=0)

    total = collect(ring_reduce(strip_of, "y"), "z")
    replicas = lax.axis_size("x") * lax.axis_size("y") * lax.axis_size("z")
    grad_wout = (total / replicas).T
    grad_ctx = jnp.dot(grad_resid, weight_t, preferred_element_type=F32).astype(BF16)
    return (grad_resid, grad_ctx, grad_wout)


def solution(mesh):
    torus = Mesh(mesh.devices.reshape(4, 4, 8, 2), ("x", "y", "z", "core"))
    dp = ("x", "y", "z")
    return jax.shard_map(
        shards,
        mesh=torus,
        in_specs=(
            P(dp, "core"),
            P(dp, None),
            P(),
            P(),
            P("core", dp),
            P(dp, None),
            P(dp),
            P(dp),
        ),
        out_specs=(P(dp, None), P(dp, "core"), P("core", dp)),
        check_vma=False,
    )
```

```python
import jax
import jax.numpy as jnp
from jax import lax
from jax.experimental import pallas as pl
from jax.experimental.pallas import tpu as pltpu
from jax.sharding import Mesh, PartitionSpec as P

F32 = jnp.float32
BF16 = jnp.bfloat16
RIGHT = [(i, (i + 1) % 4) for i in range(4)]
LEFT = [(i, (i - 1) % 4) for i in range(4)]


def norm_back(projected, residual, bias_out, norm_gain, grad_out):
    summed_in = residual.astype(F32) + projected + bias_out
    mean_in = jnp.mean(summed_in, axis=-1, keepdims=True)
    centred = summed_in - mean_in
    variance = jnp.mean(centred * centred, axis=-1, keepdims=True)
    inv_std = lax.rsqrt(variance + 1e-05)
    normed = centred * inv_std
    grad_norm = grad_out.astype(F32) * norm_gain
    first_mean = jnp.mean(grad_norm, axis=-1, keepdims=True)
    second_mean = jnp.mean(grad_norm * normed, axis=-1, keepdims=True)
    return (inv_std * (grad_norm - first_mean - normed * second_mean)).astype(BF16)


def ring_gather(piece, axis):
    mid = piece.shape[0] // 2
    before = lax.ppermute(piece, axis, RIGHT)
    after = lax.ppermute(piece, axis, LEFT)
    top = lax.ppermute(before[:mid], axis, RIGHT)
    bottom = lax.ppermute(after[mid:], axis, LEFT)
    return piece, after, top, bottom, before


def ring_reduce(chunk_of, axis):
    far = chunk_of(2).astype(BF16)
    mid = far.shape[0] // 2
    top = lax.ppermute(far[:mid], axis, RIGHT)
    bottom = lax.ppermute(far[mid:], axis, LEFT)
    ahead, behind = chunk_of(1), chunk_of(3)
    ahead = jnp.concatenate([ahead[:mid] + top.astype(F32), ahead[mid:]]).astype(BF16)
    behind = jnp.concatenate([behind[:mid], behind[mid:] + bottom.astype(F32)]).astype(BF16)
    from_before = lax.ppermute(ahead, axis, RIGHT)
    from_after = lax.ppermute(behind, axis, LEFT)
    return chunk_of(0) + from_before.astype(F32) + from_after.astype(F32)


def ring_columns(columns_of, axis):
    far = columns_of(2)
    rows = far.shape[0]
    mid = rows // 2
    right = jnp.concatenate([columns_of(1), far[:mid]])
    left = jnp.concatenate([columns_of(3), far[mid:]])
    before = lax.ppermute(right, axis, RIGHT)
    after = lax.ppermute(left, axis, LEFT)
    top = lax.ppermute(before[rows:], axis, RIGHT)
    bottom = lax.ppermute(after[rows:], axis, LEFT)
    return columns_of(0), after[:rows], top, bottom, before[:rows]


def project_kernel(*refs):
    context_ref, pieces = refs[0], refs[1:6]
    weight_ref, out_ref = refs[6], refs[7]
    ix, iy = lax.axis_index("x"), lax.axis_index("y")
    for ref, step, low in zip(pieces, (0, 1, 2, 2, 3), (0, 0, 0, 2, 0)):
        at = lax.rem(iy + step, 4)
        for k in range(ref.shape[0]):
            weight_ref[lax.rem(ix + low + k, 4), at] = ref[k]
    for x in range(4):
        block = weight_ref[x].reshape(512, 1024)
        out_ref[:, x * 512:(x + 1) * 512] = lax.dot_general(
            context_ref[...], block, (((1,), (1,)), ((), ())), preferred_element_type=F32
        )


def project(context, pieces):
    rows = context.shape[0]
    return pl.pallas_call(
        project_kernel,
        out_shape=(
            jax.ShapeDtypeStruct((4, 4, 128, 1024), BF16),
            jax.ShapeDtypeStruct((rows, 2048), F32),
        ),
        compiler_params=pltpu.CompilerParams(vmem_limit_bytes=40 << 20),
        cost_estimate=pl.CostEstimate(
            flops=2 * rows * 1024 * 2048, bytes_accessed=16 << 20, transcendentals=0
        ),
        name="project",
    )(context, *pieces)


def spread(piece, axis):
    ways = lax.axis_size(axis)
    whole = jnp.broadcast_to(piece[None], (ways,) + piece.shape)
    return lax.all_to_all(whole, axis, split_axis=0, concat_axis=0)


def collect(total, axis):
    ways = lax.axis_size(axis)
    share = total.astype(BF16).reshape(ways, -1, total.shape[1])
    got = lax.all_to_all(share, axis, split_axis=0, concat_axis=0)
    return jnp.sum(got.astype(F32), axis=0)


def shards(context, residual, bias_out, norm_gain, out_weight, cotangent, counts, slot_codes):
    capacity = slot_codes.shape[0]
    features = residual.shape[1]
    half = features // 2
    core = lax.axis_index("core")
    ix, iy = lax.axis_index("x"), lax.axis_index("y")
    live_mask = jnp.arange(capacity) < counts[0]
    swap = [(0, 1), (1, 0)]

    mine = lax.dynamic_slice_in_dim(cotangent, core * half, half, axis=1)
    weight_t = out_weight.T
    mine, weight_t = lax.optimization_barrier((mine, weight_t))
    returned = lax.all_to_all(mine, ("x", "y", "z"), split_axis=0, concat_axis=0, tiled=True)
    block = spread(weight_t, "z").reshape(128, 1024)
    context_before = lax.ppermute(context, "x", RIGHT)
    context_after = lax.ppermute(context, "x", LEFT)
    block, context_before, context_after = lax.optimization_barrier(
        (block, context_before, context_after)
    )
    mid = capacity // 2
    context_top = lax.ppermute(context_before[:mid], "x", RIGHT)
    context_bottom = lax.ppermute(context_after[mid:], "x", LEFT)
    context_pieces = (context, context_after, context_top, context_bottom, context_before)
    block = jnp.concatenate(ring_gather(block, "x")).reshape(4, 128, 1024)
    before = lax.ppermute(block, "y", RIGHT)
    after = lax.ppermute(block, "y", LEFT)
    before, after, returned = lax.optimization_barrier((before, after, returned))
    top = lax.ppermute(before[:2], "y", RIGHT)
    bottom = lax.ppermute(after[2:], "y", LEFT)
    pieces = (block, after, top, bottom, before)
    pieces, returned, context_pieces = lax.optimization_barrier((pieces, returned, context_pieces))

    weight_t, partial_proj = project(context, pieces)
    weight_t = weight_t.reshape(2048, 1024)
    picked = returned.at[slot_codes].get(mode="promise_in_bounds")
    picked = jnp.where(live_mask[:, None], picked, jnp.zeros((), picked.dtype))
    other = lax.ppermute(picked, "core", swap)
    grad_out = jnp.where(
        core == 0,
        jnp.concatenate([picked, other], axis=1),
        jnp.concatenate([other, picked], axis=1),
    )
    projected = partial_proj + lax.ppermute(partial_proj, "core", swap)
    grad_resid = norm_back(projected, residual, bias_out, norm_gain, grad_out)

    def columns_of(step):
        at = lax.rem(ix + step, 4)
        return lax.dynamic_slice_in_dim(grad_resid, at * 512, 512, axis=1)

    share = jnp.zeros((), F32)
    for columns, rows in zip(ring_columns(columns_of, "x"), context_pieces):
        share = share + lax.dot_general(
            columns, rows, (((0,), (0,)), ((), ())), preferred_element_type=F32
        )
    def strip_of(step):
        return lax.dynamic_slice_in_dim(share, lax.rem(iy + step, 4) * 128, 128, axis=0)

    total = collect(ring_reduce(strip_of, "y"), "z")
    replicas = lax.axis_size("x") * lax.axis_size("y") * lax.axis_size("z")
    grad_wout = (total / replicas).T
    grad_ctx = jnp.dot(grad_resid, weight_t, preferred_element_type=F32).astype(BF16)
    return (grad_resid, grad_ctx, grad_wout)


def solution(mesh):
    torus = Mesh(mesh.devices.reshape(4, 4, 8, 2), ("x", "y", "z", "core"))
    dp = ("x", "y", "z")
    return jax.shard_map(
        shards,
        mesh=torus,
        in_specs=(
            P(dp, "core"),
            P(dp, None),
            P(),
            P(),
            P("core", dp),
            P(dp, None),
            P(dp),
            P(dp),
        ),
        out_specs=(P(dp, None), P(dp, "core"), P("core", dp)),
        check_vma=False,
    )
```

```python
import jax
import jax.numpy as jnp
from jax import lax
from jax.experimental import pallas as pl
from jax.experimental.pallas import tpu as pltpu
from jax.sharding import Mesh, PartitionSpec as P

F32 = jnp.float32
BF16 = jnp.bfloat16
RIGHT = [(i, (i + 1) % 4) for i in range(4)]
LEFT = [(i, (i - 1) % 4) for i in range(4)]
ACROSS = [(i, (i + 2) % 4) for i in range(4)]


def norm_back(projected, residual, bias_out, norm_gain, grad_out):
    summed_in = residual.astype(F32) + projected + bias_out
    mean_in = jnp.mean(summed_in, axis=-1, keepdims=True)
    centred = summed_in - mean_in
    variance = jnp.mean(centred * centred, axis=-1, keepdims=True)
    inv_std = lax.rsqrt(variance + 1e-05)
    normed = centred * inv_std
    grad_norm = grad_out.astype(F32) * norm_gain
    first_mean = jnp.mean(grad_norm, axis=-1, keepdims=True)
    second_mean = jnp.mean(grad_norm * normed, axis=-1, keepdims=True)
    return (inv_std * (grad_norm - first_mean - normed * second_mean)).astype(BF16)


def ring_gather(piece, axis):
    mid = piece.shape[0] // 2
    before = lax.ppermute(piece, axis, RIGHT)
    after = lax.ppermute(piece, axis, LEFT)
    top = lax.ppermute(before[:mid], axis, RIGHT)
    bottom = lax.ppermute(after[mid:], axis, LEFT)
    return piece, after, top, bottom, before


def ring_reduce(chunk_of, axis):
    far = chunk_of(2).astype(BF16)
    mid = far.shape[0] // 2
    top = lax.ppermute(far[:mid], axis, RIGHT)
    bottom = lax.ppermute(far[mid:], axis, LEFT)
    ahead, behind = chunk_of(1), chunk_of(3)
    ahead = jnp.concatenate([ahead[:mid] + top.astype(F32), ahead[mid:]]).astype(BF16)
    behind = jnp.concatenate([behind[:mid], behind[mid:] + bottom.astype(F32)]).astype(BF16)
    from_before = lax.ppermute(ahead, axis, RIGHT)
    from_after = lax.ppermute(behind, axis, LEFT)
    return chunk_of(0) + from_before.astype(F32) + from_after.astype(F32)


def ring_reduce(chunk_of, axis):
    far = chunk_of(2).astype(BF16)
    mid = far.shape[0] // 2
    top = lax.ppermute(far[:mid], axis, RIGHT)
    bottom = lax.ppermute(far[mid:], axis, LEFT)
    ahead, behind = chunk_of(1), chunk_of(3)
    ahead = jnp.concatenate([ahead[:mid] + top.astype(F32), ahead[mid:]]).astype(BF16)
    behind = jnp.concatenate([behind[:mid], behind[mid:] + bottom.astype(F32)]).astype(BF16)
    from_before = lax.ppermute(ahead, axis, RIGHT)
    from_after = lax.ppermute(behind, axis, LEFT)
    return chunk_of(0) + from_before.astype(F32) + from_after.astype(F32)


def ring_columns(columns_of, axis):
    far = columns_of(2)
    rows = far.shape[0]
    mid = rows // 2
    right = jnp.concatenate([columns_of(1), far[:mid]])
    left = jnp.concatenate([columns_of(3), far[mid:]])
    before = lax.ppermute(right, axis, RIGHT)
    after = lax.ppermute(left, axis, LEFT)
    top = lax.ppermute(before[rows:], axis, RIGHT)
    bottom = lax.ppermute(after[rows:], axis, LEFT)
    return columns_of(0), after[:rows], top, bottom, before[:rows]


def project_kernel(*refs):
    context_ref, pieces = refs[0], refs[1:6]
    weight_ref, out_ref = refs[6], refs[7]
    placed, sems = refs[8], refs[9]
    ix, iy = lax.axis_index("x"), lax.axis_index("y")
    for ref, step, low in zip(pieces, (0, 1, 2, 2, 3), (0, 0, 0, 2, 0)):
        at = lax.rem(iy + step, 4)
        for k in range(ref.shape[0]):
            placed[lax.rem(ix + low + k, 4), at] = ref[k]
    copies = [
        pltpu.make_async_copy(placed.at[x], weight_ref.at[x], sems.at[x]) for x in range(4)
    ]
    for copy in copies:
        copy.start()
    for x in range(4):
        block = placed[x].reshape(512, 1024)
        out_ref[:, x * 512:(x + 1) * 512] = lax.dot_general(
            context_ref[...], block, (((1,), (1,)), ((), ())), preferred_element_type=F32
        )
    for copy in copies:
        copy.wait()


def project(context, pieces):
    rows = context.shape[0]
    vmem = pl.BlockSpec(memory_space=pltpu.VMEM)
    return pl.pallas_call(
        project_kernel,
        out_shape=(
            jax.ShapeDtypeStruct((4, 4, 128, 1024), BF16),
            jax.ShapeDtypeStruct((rows, 2048), F32),
        ),
        in_specs=[vmem] * 6,
        out_specs=(pl.BlockSpec(memory_space=pltpu.HBM), vmem),
        scratch_shapes=[
            pltpu.VMEM((4, 4, 128, 1024), BF16),
            pltpu.SemaphoreType.DMA((4,)),
        ],
        compiler_params=pltpu.CompilerParams(vmem_limit_bytes=40 << 20),
        cost_estimate=pl.CostEstimate(
            flops=2 * rows * 1024 * 2048, bytes_accessed=16 << 20, transcendentals=0
        ),
        name="project",
    )(context, *pieces)


def spread(piece, axis):
    ways = lax.axis_size(axis)
    whole = jnp.broadcast_to(piece[None], (ways,) + piece.shape)
    return lax.all_to_all(whole, axis, split_axis=0, concat_axis=0)


def collect(total, axis):
    ways = lax.axis_size(axis)
    share = total.astype(BF16).reshape(ways, -1, total.shape[1])
    got = lax.all_to_all(share, axis, split_axis=0, concat_axis=0)
    return jnp.sum(got.astype(F32), axis=0)


def shards(context, residual, bias_out, norm_gain, out_weight, cotangent, counts, slot_codes):
    capacity = slot_codes.shape[0]
    features = residual.shape[1]
    half = features // 2
    core = lax.axis_index("core")
    ix, iy = lax.axis_index("x"), lax.axis_index("y")
    live_mask = jnp.arange(capacity) < counts[0]
    swap = [(0, 1), (1, 0)]

    mine = lax.dynamic_slice_in_dim(cotangent, core * half, half, axis=1)
    weight_t = out_weight.T
    mine, weight_t = lax.optimization_barrier((mine, weight_t))
    returned = lax.all_to_all(mine, ("x", "y", "z"), split_axis=0, concat_axis=0, tiled=True)
    block = spread(weight_t, "z").reshape(128, 1024)
    context_before = lax.ppermute(context, "x", RIGHT)
    context_after = lax.ppermute(context, "x", LEFT)
    block, context_before, context_after = lax.optimization_barrier(
        (block, context_before, context_after)
    )
    mid = capacity // 2
    context_top = lax.ppermute(context_before[:mid], "x", RIGHT)
    context_bottom = lax.ppermute(context_after[mid:], "x", LEFT)
    context_pieces = (context, context_after, context_top, context_bottom, context_before)
    block = jnp.concatenate(ring_gather(block, "x")).reshape(4, 128, 1024)
    before = lax.ppermute(block, "y", RIGHT)
    after = lax.ppermute(block, "y", LEFT)
    before, after, context_pieces = lax.optimization_barrier((before, after, context_pieces))
    top = lax.ppermute(before[:2], "y", RIGHT)
    bottom = lax.ppermute(after[2:], "y", LEFT)
    pieces = (block, after, top, bottom, before)
    pieces, returned = lax.optimization_barrier((pieces, returned))

    weight_t, partial_proj = project(context, pieces)
    weight_t = weight_t.reshape(2048, 1024)
    picked = returned.at[slot_codes].get(mode="promise_in_bounds")
    picked = jnp.where(live_mask[:, None], picked, jnp.zeros((), picked.dtype))
    other = lax.ppermute(picked, "core", swap)
    grad_out = jnp.where(
        core == 0,
        jnp.concatenate([picked, other], axis=1),
        jnp.concatenate([other, picked], axis=1),
    )
    projected = partial_proj + lax.ppermute(partial_proj, "core", swap)
    grad_resid = norm_back(projected, residual, bias_out, norm_gain, grad_out)

    def columns_of(step):
        at = lax.rem(ix + step, 4)
        return lax.dynamic_slice_in_dim(grad_resid, at * 512, 512, axis=1)

    def product(columns, rows):
        return lax.dot_general(
            columns, rows, (((0,), (0,)), ((), ())), preferred_element_type=F32
        )

    def half_of(step):
        at = lax.rem(ix + step, 4)
        return lax.dynamic_slice(grad_resid, (core * mid, at * 512), (mid, 512))

    fetched = jnp.concatenate([
        lax.ppermute(half_of(3), "x", LEFT),
        lax.ppermute(half_of(2), "x", ACROSS),
        lax.ppermute(half_of(1), "x", RIGHT),
    ])
    swapped = lax.ppermute(fetched, "core", swap)
    far_rows = jnp.concatenate(context_pieces[2:4])
    three = (context_pieces[1], far_rows, context_pieces[4])

    def halves(which):
        return jnp.concatenate(
            [lax.dynamic_slice_in_dim(rows, which * mid, mid, axis=0) for rows in three]
        )

    share = product(columns_of(0), context)
    share = share + product(fetched, halves(core))
    share = share + product(swapped, halves(1 - core))

    def strip_of(step):
        return lax.dynamic_slice_in_dim(share, lax.rem(iy + step, 4) * 128, 128, axis=0)

    total = collect(ring_reduce(strip_of, "y"), "z")
    replicas = lax.axis_size("x") * lax.axis_size("y") * lax.axis_size("z")
    grad_wout = (total / replicas).T
    grad_ctx = jnp.dot(grad_resid, weight_t, preferred_element_type=F32).astype(BF16)
    return (grad_resid, grad_ctx, grad_wout)


def solution(mesh):
    torus = Mesh(mesh.devices.reshape(4, 4, 8, 2), ("x", "y", "z", "core"))
    dp = ("x", "y", "z")
    return jax.shard_map(
        shards,
        mesh=torus,
        in_specs=(
            P(dp, "core"),
            P(dp, None),
            P(),
            P(),
            P("core", dp),
            P(dp, None),
            P(dp),
            P(dp),
        ),
        out_specs=(P(dp, None), P(dp, "core"), P("core", dp)),
        check_vma=False,
    )
```

```python
import jax
import jax.numpy as jnp
from jax import lax
from jax.experimental import pallas as pl
from jax.experimental.pallas import tpu as pltpu
from jax.sharding import Mesh, PartitionSpec as P

F32 = jnp.float32
BF16 = jnp.bfloat16
RIGHT = [(i, (i + 1) % 4) for i in range(4)]
LEFT = [(i, (i - 1) % 4) for i in range(4)]
ACROSS = [(i, (i + 2) % 4) for i in range(4)]


def norm_kernel(own_ref, other_ref, residual_ref, bias_ref, gain_ref, low_ref, high_ref, out_ref):
    summed_in = residual_ref[...].astype(F32) + (own_ref[...] + other_ref[...]) + bias_ref[...]
    mean_in = jnp.mean(summed_in, axis=-1, keepdims=True)
    centred = summed_in - mean_in
    variance = jnp.mean(centred * centred, axis=-1, keepdims=True)
    inv_std = lax.rsqrt(variance + 1e-05)
    normed = centred * inv_std
    grad_out = jnp.concatenate([low_ref[...], high_ref[...]], axis=1)
    grad_norm = grad_out.astype(F32) * gain_ref[...]
    first_mean = jnp.mean(grad_norm, axis=-1, keepdims=True)
    second_mean = jnp.mean(grad_norm * normed, axis=-1, keepdims=True)
    out_ref[...] = (inv_std * (grad_norm - first_mean - normed * second_mean)).astype(BF16)


def norm_back(own, other, residual, bias_out, norm_gain, low, high):
    rows, features = residual.shape
    step = 64
    wide = pl.BlockSpec((step, features), lambda i: (i, 0))
    narrow = pl.BlockSpec((step, features // 2), lambda i: (i, 0))
    single = pl.BlockSpec((1, features), lambda i: (0, 0))
    return pl.pallas_call(
        norm_kernel,
        grid=(rows // step,),
        out_shape=jax.ShapeDtypeStruct((rows, features), BF16),
        in_specs=[wide, wide, wide, single, single, narrow, narrow],
        out_specs=wide,
        compiler_params=pltpu.CompilerParams(vmem_limit_bytes=24 << 20),
        cost_estimate=pl.CostEstimate(
            flops=20 * rows * features, bytes_accessed=14 * rows * features, transcendentals=rows
        ),
        name="norm_back",
    )(own, other, residual, bias_out[None], norm_gain[None], low, high)


def order_kernel(*refs):
    iz = lax.axis_index("z")
    out_ref = refs[-1]
    for step, ref in enumerate(refs[:-1]):
        out_ref[lax.rem(iz + step, 8)] = ref[...]


def gather_z(piece):
    pieces = [piece] + [
        lax.ppermute(piece, "z", [(i, (i - step) % 8) for i in range(8)]) for step in range(1, 8)
    ]
    vmem = pl.BlockSpec(memory_space=pltpu.VMEM)
    return pl.pallas_call(
        order_kernel,
        out_shape=jax.ShapeDtypeStruct((8,) + piece.shape, piece.dtype),
        in_specs=[vmem] * 8,
        out_specs=vmem,
        cost_estimate=pl.CostEstimate(flops=0, bytes_accessed=1 << 19, transcendentals=0),
        name="order_z",
    )(*pieces)


def ring_gather(piece, axis):
    mid = piece.shape[0] // 2
    before = lax.ppermute(piece, axis, RIGHT)
    after = lax.ppermute(piece, axis, LEFT)
    top = lax.ppermute(before[:mid], axis, RIGHT)
    bottom = lax.ppermute(after[mid:], axis, LEFT)
    return piece, after, top, bottom, before


def ring_reduce(chunk_of, axis):
    far = chunk_of(2).astype(BF16)
    mid = far.shape[0] // 2
    top = lax.ppermute(far[:mid], axis, RIGHT)
    bottom = lax.ppermute(far[mid:], axis, LEFT)
    ahead, behind = chunk_of(1), chunk_of(3)
    ahead = jnp.concatenate([ahead[:mid] + top.astype(F32), ahead[mid:]]).astype(BF16)
    behind = jnp.concatenate([behind[:mid], behind[mid:] + bottom.astype(F32)]).astype(BF16)
    from_before = lax.ppermute(ahead, axis, RIGHT)
    from_after = lax.ppermute(behind, axis, LEFT)
    return chunk_of(0) + from_before.astype(F32) + from_after.astype(F32)


def ring_reduce(chunk_of, axis):
    far = chunk_of(2).astype(BF16)
    mid = far.shape[0] // 2
    top = lax.ppermute(far[:mid], axis, RIGHT)
    bottom = lax.ppermute(far[mid:], axis, LEFT)
    ahead, behind = chunk_of(1), chunk_of(3)
    ahead = jnp.concatenate([ahead[:mid] + top.astype(F32), ahead[mid:]]).astype(BF16)
    behind = jnp.concatenate([behind[:mid], behind[mid:] + bottom.astype(F32)]).astype(BF16)
    from_before = lax.ppermute(ahead, axis, RIGHT)
    from_after = lax.ppermute(behind, axis, LEFT)
    return chunk_of(0) + from_before.astype(F32) + from_after.astype(F32)


def ring_columns(columns_of, axis):
    far = columns_of(2)
    rows = far.shape[0]
    mid = rows // 2
    right = jnp.concatenate([columns_of(1), far[:mid]])
    left = jnp.concatenate([columns_of(3), far[mid:]])
    before = lax.ppermute(right, axis, RIGHT)
    after = lax.ppermute(left, axis, LEFT)
    top = lax.ppermute(before[rows:], axis, RIGHT)
    bottom = lax.ppermute(after[rows:], axis, LEFT)
    return columns_of(0), after[:rows], top, bottom, before[:rows]


def project_kernel(*refs):
    context_ref, pieces = refs[0], refs[1:6]
    weight_ref, out_ref = refs[6], refs[7]
    placed, sems = refs[8], refs[9]
    ix, iy = lax.axis_index("x"), lax.axis_index("y")
    for ref, step, low in zip(pieces, (0, 1, 2, 2, 3), (0, 0, 0, 2, 0)):
        at = lax.rem(iy + step, 4)
        for k in range(ref.shape[0]):
            placed[lax.rem(ix + low + k, 4), at] = ref[k]
    copies = [
        pltpu.make_async_copy(placed.at[x], weight_ref.at[x], sems.at[x]) for x in range(4)
    ]
    for copy in copies:
        copy.start()
    for x in range(4):
        block = placed[x].reshape(512, 1024)
        out_ref[:, x * 512:(x + 1) * 512] = lax.dot_general(
            context_ref[...], block, (((1,), (1,)), ((), ())), preferred_element_type=F32
        )
    for copy in copies:
        copy.wait()


def project(context, pieces):
    rows = context.shape[0]
    vmem = pl.BlockSpec(memory_space=pltpu.VMEM)
    return pl.pallas_call(
        project_kernel,
        out_shape=(
            jax.ShapeDtypeStruct((4, 4, 128, 1024), BF16),
            jax.ShapeDtypeStruct((rows, 2048), F32),
        ),
        in_specs=[vmem] * 6,
        out_specs=(pl.BlockSpec(memory_space=pltpu.HBM), vmem),
        scratch_shapes=[
            pltpu.VMEM((4, 4, 128, 1024), BF16),
            pltpu.SemaphoreType.DMA((4,)),
        ],
        compiler_params=pltpu.CompilerParams(vmem_limit_bytes=40 << 20),
        cost_estimate=pl.CostEstimate(
            flops=2 * rows * 1024 * 2048, bytes_accessed=16 << 20, transcendentals=0
        ),
        name="project",
    )(context, *pieces)


def collect(total, axis):
    ways = lax.axis_size(axis)
    share = total.astype(BF16).reshape(ways, -1, total.shape[1])
    got = lax.all_to_all(share, axis, split_axis=0, concat_axis=0)
    return jnp.sum(got.astype(F32), axis=0)


def shards(context, residual, bias_out, norm_gain, out_weight, cotangent, counts, slot_codes):
    capacity = slot_codes.shape[0]
    features = residual.shape[1]
    half = features // 2
    core = lax.axis_index("core")
    ix, iy = lax.axis_index("x"), lax.axis_index("y")
    live_mask = jnp.arange(capacity) < counts[0]
    swap = [(0, 1), (1, 0)]

    mine = lax.dynamic_slice_in_dim(cotangent, core * half, half, axis=1)
    weight_t = out_weight.T
    mine, weight_t = lax.optimization_barrier((mine, weight_t))
    returned = lax.all_to_all(mine, ("x", "y", "z"), split_axis=0, concat_axis=0, tiled=True)
    block = gather_z(weight_t).reshape(128, 1024)
    context_before = lax.ppermute(context, "x", RIGHT)
    context_after = lax.ppermute(context, "x", LEFT)
    block, context_before, context_after = lax.optimization_barrier(
        (block, context_before, context_after)
    )
    mid = capacity // 2
    context_top = lax.ppermute(context_before[:mid], "x", RIGHT)
    context_bottom = lax.ppermute(context_after[mid:], "x", LEFT)
    context_pieces = (context, context_after, context_top, context_bottom, context_before)
    block = jnp.concatenate(ring_gather(block, "x")).reshape(4, 128, 1024)
    before = lax.ppermute(block, "y", RIGHT)
    after = lax.ppermute(block, "y", LEFT)
    before, after, context_pieces = lax.optimization_barrier((before, after, context_pieces))
    top = lax.ppermute(before[:2], "y", RIGHT)
    bottom = lax.ppermute(after[2:], "y", LEFT)
    pieces = (block, after, top, bottom, before)
    pieces, returned = lax.optimization_barrier((pieces, returned))

    weight_t, partial_proj = project(context, pieces)
    weight_t = weight_t.reshape(2048, 1024)
    picked = returned.at[slot_codes].get(mode="promise_in_bounds")
    picked = jnp.where(live_mask[:, None], picked, jnp.zeros((), picked.dtype))
    other = lax.ppermute(picked, "core", swap)
    low = jnp.where(core == 0, picked, other)
    high = jnp.where(core == 0, other, picked)
    theirs = lax.ppermute(partial_proj, "core", swap)
    grad_resid = norm_back(partial_proj, theirs, residual, bias_out, norm_gain, low, high)

    def columns_of(step):
        at = lax.rem(ix + step, 4)
        return lax.dynamic_slice_in_dim(grad_resid, at * 512, 512, axis=1)

    def product(columns, rows):
        return lax.dot_general(
            columns, rows, (((0,), (0,)), ((), ())), preferred_element_type=F32
        )

    def half_of(step):
        at = lax.rem(ix + step, 4)
        return lax.dynamic_slice(grad_resid, (core * mid, at * 512), (mid, 512))

    fetched = jnp.concatenate([
        lax.ppermute(half_of(3), "x", LEFT),
        lax.ppermute(half_of(2), "x", ACROSS),
        lax.ppermute(half_of(1), "x", RIGHT),
    ])
    swapped = lax.ppermute(fetched, "core", swap)
    far_rows = jnp.concatenate(context_pieces[2:4])
    three = (context_pieces[1], far_rows, context_pieces[4])

    def halves(which):
        return jnp.concatenate(
            [lax.dynamic_slice_in_dim(rows, which * mid, mid, axis=0) for rows in three]
        )

    share = product(columns_of(0), context)
    share = share + product(fetched, halves(core))
    share = share + product(swapped, halves(1 - core))

    def strip_of(step):
        return lax.dynamic_slice_in_dim(share, lax.rem(iy + step, 4) * 128, 128, axis=0)

    total = collect(ring_reduce(strip_of, "y"), "z")
    replicas = lax.axis_size("x") * lax.axis_size("y") * lax.axis_size("z")
    grad_wout = (total / replicas).T
    grad_ctx = jnp.dot(grad_resid, weight_t, preferred_element_type=F32).astype(BF16)
    return (grad_resid, grad_ctx, grad_wout)


def solution(mesh):
    torus = Mesh(mesh.devices.reshape(4, 4, 8, 2), ("x", "y", "z", "core"))
    dp = ("x", "y", "z")
    return jax.shard_map(
        shards,
        mesh=torus,
        in_specs=(
            P(dp, "core"),
            P(dp, None),
            P(),
            P(),
            P("core", dp),
            P(dp, None),
            P(dp),
            P(dp),
        ),
        out_specs=(P(dp, None), P(dp, "core"), P("core", dp)),
        check_vma=False,
    )
```

```python
import jax
import jax.numpy as jnp
from jax import lax
from jax.experimental import pallas as pl
from jax.experimental.pallas import tpu as pltpu
from jax.sharding import Mesh, PartitionSpec as P

F32 = jnp.float32
BF16 = jnp.bfloat16
RIGHT = [(i, (i + 1) % 4) for i in range(4)]
LEFT = [(i, (i - 1) % 4) for i in range(4)]
ACROSS = [(i, (i + 2) % 4) for i in range(4)]


def norm_back(projected, residual, bias_out, norm_gain, grad_out):
    summed_in = residual.astype(F32) + projected + bias_out
    mean_in = jnp.mean(summed_in, axis=-1, keepdims=True)
    centred = summed_in - mean_in
    variance = jnp.mean(centred * centred, axis=-1, keepdims=True)
    inv_std = lax.rsqrt(variance + 1e-05)
    normed = centred * inv_std
    grad_norm = grad_out.astype(F32) * norm_gain
    first_mean = jnp.mean(grad_norm, axis=-1, keepdims=True)
    second_mean = jnp.mean(grad_norm * normed, axis=-1, keepdims=True)
    return (inv_std * (grad_norm - first_mean - normed * second_mean)).astype(BF16)


def ring_gather(piece, axis):
    mid = piece.shape[0] // 2
    before = lax.ppermute(piece, axis, RIGHT)
    after = lax.ppermute(piece, axis, LEFT)
    top = lax.ppermute(before[:mid], axis, RIGHT)
    bottom = lax.ppermute(after[mid:], axis, LEFT)
    return piece, after, top, bottom, before


def ring_reduce(chunk_of, axis):
    far = chunk_of(2).astype(BF16)
    mid = far.shape[0] // 2
    top = lax.ppermute(far[:mid], axis, RIGHT)
    bottom = lax.ppermute(far[mid:], axis, LEFT)
    ahead, behind = chunk_of(1), chunk_of(3)
    ahead = jnp.concatenate([ahead[:mid] + top.astype(F32), ahead[mid:]]).astype(BF16)
    behind = jnp.concatenate([behind[:mid], behind[mid:] + bottom.astype(F32)]).astype(BF16)
    from_before = lax.ppermute(ahead, axis, RIGHT)
    from_after = lax.ppermute(behind, axis, LEFT)
    return chunk_of(0) + from_before.astype(F32) + from_after.astype(F32)


def ring_reduce(chunk_of, axis):
    far = chunk_of(2).astype(BF16)
    mid = far.shape[0] // 2
    top = lax.ppermute(far[:mid], axis, RIGHT)
    bottom = lax.ppermute(far[mid:], axis, LEFT)
    ahead, behind = chunk_of(1), chunk_of(3)
    ahead = jnp.concatenate([ahead[:mid] + top.astype(F32), ahead[mid:]]).astype(BF16)
    behind = jnp.concatenate([behind[:mid], behind[mid:] + bottom.astype(F32)]).astype(BF16)
    from_before = lax.ppermute(ahead, axis, RIGHT)
    from_after = lax.ppermute(behind, axis, LEFT)
    return chunk_of(0) + from_before.astype(F32) + from_after.astype(F32)


def ring_columns(columns_of, axis):
    far = columns_of(2)
    rows = far.shape[0]
    mid = rows // 2
    right = jnp.concatenate([columns_of(1), far[:mid]])
    left = jnp.concatenate([columns_of(3), far[mid:]])
    before = lax.ppermute(right, axis, RIGHT)
    after = lax.ppermute(left, axis, LEFT)
    top = lax.ppermute(before[rows:], axis, RIGHT)
    bottom = lax.ppermute(after[rows:], axis, LEFT)
    return columns_of(0), after[:rows], top, bottom, before[:rows]


def project_kernel(*refs):
    context_ref, pieces = refs[0], refs[1:6]
    weight_ref, out_ref = refs[6], refs[7]
    placed, sems = refs[8], refs[9]
    ix, iy = lax.axis_index("x"), lax.axis_index("y")
    for ref, step, low in zip(pieces, (0, 1, 2, 2, 3), (0, 0, 0, 2, 0)):
        at = lax.rem(iy + step, 4)
        for k in range(ref.shape[0]):
            placed[lax.rem(ix + low + k, 4), at] = ref[k]
    copies = [
        pltpu.make_async_copy(placed.at[x], weight_ref.at[x], sems.at[x]) for x in range(4)
    ]
    for copy in copies:
        copy.start()
    for x in range(4):
        block = placed[x].reshape(512, 1024)
        out_ref[:, x * 512:(x + 1) * 512] = lax.dot_general(
            context_ref[...], block, (((1,), (1,)), ((), ())), preferred_element_type=F32
        )
    for copy in copies:
        copy.wait()


def project(context, pieces):
    rows = context.shape[0]
    vmem = pl.BlockSpec(memory_space=pltpu.VMEM)
    return pl.pallas_call(
        project_kernel,
        out_shape=(
            jax.ShapeDtypeStruct((4, 4, 128, 1024), BF16),
            jax.ShapeDtypeStruct((rows, 2048), F32),
        ),
        in_specs=[vmem] * 6,
        out_specs=(pl.BlockSpec(memory_space=pltpu.HBM), vmem),
        scratch_shapes=[
            pltpu.VMEM((4, 4, 128, 1024), BF16),
            pltpu.SemaphoreType.DMA((4,)),
        ],
        compiler_params=pltpu.CompilerParams(vmem_limit_bytes=40 << 20),
        cost_estimate=pl.CostEstimate(
            flops=2 * rows * 1024 * 2048, bytes_accessed=16 << 20, transcendentals=0
        ),
        name="project",
    )(context, *pieces)


def spread(piece, axis):
    ways = lax.axis_size(axis)
    whole = jnp.broadcast_to(piece[None], (ways,) + piece.shape)
    return lax.all_to_all(whole, axis, split_axis=0, concat_axis=0)


def collect(total, axis):
    ways = lax.axis_size(axis)
    share = total.astype(BF16).reshape(ways, -1, total.shape[1])
    got = lax.all_to_all(share, axis, split_axis=0, concat_axis=0)
    return jnp.sum(got.astype(F32), axis=0)


def shards(context, residual, bias_out, norm_gain, out_weight, cotangent, counts, slot_codes):
    capacity = slot_codes.shape[0]
    features = residual.shape[1]
    half = features // 2
    core = lax.axis_index("core")
    ix, iy = lax.axis_index("x"), lax.axis_index("y")
    live_mask = jnp.arange(capacity) < counts[0]
    swap = [(0, 1), (1, 0)]

    mine = lax.dynamic_slice_in_dim(cotangent, core * half, half, axis=1)
    weight_t = out_weight.T
    mine, weight_t = lax.optimization_barrier((mine, weight_t))
    returned = lax.all_to_all(mine, ("x", "y", "z"), split_axis=0, concat_axis=0, tiled=True)
    block = spread(weight_t, "z").reshape(128, 1024)
    block = jnp.concatenate(ring_gather(block, "x")).reshape(4, 128, 1024)
    block, held = lax.optimization_barrier((block, context))
    context_before = lax.ppermute(held, "x", RIGHT)
    context_after = lax.ppermute(held, "x", LEFT)
    before = lax.ppermute(block, "y", RIGHT)
    after = lax.ppermute(block, "y", LEFT)
    mid = capacity // 2
    top = lax.ppermute(before[:2], "y", RIGHT)
    bottom = lax.ppermute(after[2:], "y", LEFT)
    pieces = (block, after, top, bottom, before)
    pieces, returned, context_before, context_after = lax.optimization_barrier(
        (pieces, returned, context_before, context_after)
    )
    context_top = lax.ppermute(context_before[:mid], "x", RIGHT)
    context_bottom = lax.ppermute(context_after[mid:], "x", LEFT)

    weight_t, partial_proj = project(context, pieces)
    weight_t = weight_t.reshape(2048, 1024)
    picked = returned.at[slot_codes].get(mode="promise_in_bounds")
    picked = jnp.where(live_mask[:, None], picked, jnp.zeros((), picked.dtype))
    other = lax.ppermute(picked, "core", swap)
    grad_out = jnp.where(
        core == 0,
        jnp.concatenate([picked, other], axis=1),
        jnp.concatenate([other, picked], axis=1),
    )
    theirs = lax.ppermute(partial_proj, "core", swap)
    context_pieces = (context, context_after, context_top, context_bottom, context_before)
    theirs, context_pieces = lax.optimization_barrier((theirs, context_pieces))
    projected = partial_proj + theirs
    grad_resid = norm_back(projected, residual, bias_out, norm_gain, grad_out)

    def columns_of(step):
        at = lax.rem(ix + step, 4)
        return lax.dynamic_slice_in_dim(grad_resid, at * 512, 512, axis=1)

    def product(columns, rows):
        return lax.dot_general(
            columns, rows, (((0,), (0,)), ((), ())), preferred_element_type=F32
        )

    def half_of(step):
        at = lax.rem(ix + step, 4)
        return lax.dynamic_slice(grad_resid, (core * mid, at * 512), (mid, 512))

    fetched = jnp.concatenate([
        lax.ppermute(half_of(3), "x", LEFT),
        lax.ppermute(half_of(2), "x", ACROSS),
        lax.ppermute(half_of(1), "x", RIGHT),
    ])
    swapped = lax.ppermute(fetched, "core", swap)
    far_rows = jnp.concatenate(context_pieces[2:4])
    three = (context_pieces[1], far_rows, context_pieces[4])

    def halves(which):
        return jnp.concatenate(
            [lax.dynamic_slice_in_dim(rows, which * mid, mid, axis=0) for rows in three]
        )

    share = product(columns_of(0), context)
    share = share + product(fetched, halves(core))
    share = share + product(swapped, halves(1 - core))

    def strip_of(step):
        return lax.dynamic_slice_in_dim(share, lax.rem(iy + step, 4) * 128, 128, axis=0)

    total = collect(ring_reduce(strip_of, "y"), "z")
    replicas = lax.axis_size("x") * lax.axis_size("y") * lax.axis_size("z")
    grad_wout = (total / replicas).T
    grad_ctx = jnp.dot(grad_resid, weight_t, preferred_element_type=F32).astype(BF16)
    return (grad_resid, grad_ctx, grad_wout)


def solution(mesh):
    torus = Mesh(mesh.devices.reshape(4, 4, 8, 2), ("x", "y", "z", "core"))
    dp = ("x", "y", "z")
    return jax.shard_map(
        shards,
        mesh=torus,
        in_specs=(
            P(dp, "core"),
            P(dp, None),
            P(),
            P(),
            P("core", dp),
            P(dp, None),
            P(dp),
            P(dp),
        ),
        out_specs=(P(dp, None), P(dp, "core"), P("core", dp)),
        check_vma=False,
    )
```

```python
import jax
import jax.numpy as jnp
from jax import lax
from jax.experimental import pallas as pl
from jax.experimental.pallas import tpu as pltpu
from jax.sharding import Mesh, PartitionSpec as P

F32 = jnp.float32
BF16 = jnp.bfloat16
RIGHT = [(i, (i + 1) % 4) for i in range(4)]
LEFT = [(i, (i - 1) % 4) for i in range(4)]
ACROSS = [(i, (i + 2) % 4) for i in range(4)]


def norm_back(projected, residual, bias_out, norm_gain, grad_out):
    summed_in = residual.astype(F32) + projected + bias_out
    mean_in = jnp.mean(summed_in, axis=-1, keepdims=True)
    centred = summed_in - mean_in
    variance = jnp.mean(centred * centred, axis=-1, keepdims=True)
    inv_std = lax.rsqrt(variance + 1e-05)
    normed = centred * inv_std
    grad_norm = grad_out.astype(F32) * norm_gain
    first_mean = jnp.mean(grad_norm, axis=-1, keepdims=True)
    second_mean = jnp.mean(grad_norm * normed, axis=-1, keepdims=True)
    return (inv_std * (grad_norm - first_mean - normed * second_mean)).astype(BF16)


def ring_gather(piece, axis):
    mid = piece.shape[0] // 2
    before = lax.ppermute(piece, axis, RIGHT)
    after = lax.ppermute(piece, axis, LEFT)
    top = lax.ppermute(before[:mid], axis, RIGHT)
    bottom = lax.ppermute(after[mid:], axis, LEFT)
    return piece, after, top, bottom, before


def ring_reduce(chunk_of, axis):
    far = chunk_of(2).astype(BF16)
    mid = far.shape[0] // 2
    top = lax.ppermute(far[:mid], axis, RIGHT)
    bottom = lax.ppermute(far[mid:], axis, LEFT)
    ahead, behind = chunk_of(1), chunk_of(3)
    ahead = jnp.concatenate([ahead[:mid] + top.astype(F32), ahead[mid:]]).astype(BF16)
    behind = jnp.concatenate([behind[:mid], behind[mid:] + bottom.astype(F32)]).astype(BF16)
    from_before = lax.ppermute(ahead, axis, RIGHT)
    from_after = lax.ppermute(behind, axis, LEFT)
    return chunk_of(0) + from_before.astype(F32) + from_after.astype(F32)


def ring_reduce(chunk_of, axis):
    far = chunk_of(2).astype(BF16)
    mid = far.shape[0] // 2
    top = lax.ppermute(far[:mid], axis, RIGHT)
    bottom = lax.ppermute(far[mid:], axis, LEFT)
    ahead, behind = chunk_of(1), chunk_of(3)
    ahead = jnp.concatenate([ahead[:mid] + top.astype(F32), ahead[mid:]]).astype(BF16)
    behind = jnp.concatenate([behind[:mid], behind[mid:] + bottom.astype(F32)]).astype(BF16)
    from_before = lax.ppermute(ahead, axis, RIGHT)
    from_after = lax.ppermute(behind, axis, LEFT)
    return chunk_of(0) + from_before.astype(F32) + from_after.astype(F32)


def ring_columns(columns_of, axis):
    far = columns_of(2)
    rows = far.shape[0]
    mid = rows // 2
    right = jnp.concatenate([columns_of(1), far[:mid]])
    left = jnp.concatenate([columns_of(3), far[mid:]])
    before = lax.ppermute(right, axis, RIGHT)
    after = lax.ppermute(left, axis, LEFT)
    top = lax.ppermute(before[rows:], axis, RIGHT)
    bottom = lax.ppermute(after[rows:], axis, LEFT)
    return columns_of(0), after[:rows], top, bottom, before[:rows]


def project_kernel(*refs):
    context_ref, a_pieces, b_pieces = refs[0], refs[1:6], refs[6:11]
    weight_ref, out_ref = refs[11], refs[12]
    placed, sems = refs[13], refs[14]
    ix, iy = lax.axis_index("x"), lax.axis_index("y")
    steps, lows = (0, 1, 2, 2, 3), (0, 0, 0, 2, 0)
    for ref, step, low in zip(a_pieces, steps, lows):
        for k in range(ref.shape[0]):
            placed[lax.rem(ix + step, 4), lax.rem(iy + low + k, 4), :, 0:512] = ref[k]
    for ref, step, low in zip(b_pieces, steps, lows):
        for k in range(ref.shape[0]):
            placed[lax.rem(ix + low + k, 4), lax.rem(iy + step, 4), :, 512:1024] = ref[k]
    copies = [
        pltpu.make_async_copy(placed.at[x], weight_ref.at[x], sems.at[x]) for x in range(4)
    ]
    for copy in copies:
        copy.start()
    for x in range(4):
        block = placed[x].reshape(512, 1024)
        out_ref[:, x * 512:(x + 1) * 512] = lax.dot_general(
            context_ref[...], block, (((1,), (1,)), ((), ())), preferred_element_type=F32
        )
    for copy in copies:
        copy.wait()


def project(context, pieces):
    rows = context.shape[0]
    vmem = pl.BlockSpec(memory_space=pltpu.VMEM)
    return pl.pallas_call(
        project_kernel,
        out_shape=(
            jax.ShapeDtypeStruct((4, 4, 128, 1024), BF16),
            jax.ShapeDtypeStruct((rows, 2048), F32),
        ),
        in_specs=[vmem] * 11,
        out_specs=(pl.BlockSpec(memory_space=pltpu.HBM), vmem),
        scratch_shapes=[
            pltpu.VMEM((4, 4, 128, 1024), BF16),
            pltpu.SemaphoreType.DMA((4,)),
        ],
        compiler_params=pltpu.CompilerParams(vmem_limit_bytes=40 << 20),
        cost_estimate=pl.CostEstimate(
            flops=2 * rows * 1024 * 2048, bytes_accessed=16 << 20, transcendentals=0
        ),
        name="project",
    )(context, *pieces)


def spread(piece, axis):
    ways = lax.axis_size(axis)
    whole = jnp.broadcast_to(piece[None], (ways,) + piece.shape)
    return lax.all_to_all(whole, axis, split_axis=0, concat_axis=0)


def collect(total, axis):
    ways = lax.axis_size(axis)
    share = total.astype(BF16).reshape(ways, -1, total.shape[1])
    got = lax.all_to_all(share, axis, split_axis=0, concat_axis=0)
    return jnp.sum(got.astype(F32), axis=0)


def shards(context, residual, bias_out, norm_gain, out_weight, cotangent, counts, slot_codes):
    capacity = slot_codes.shape[0]
    features = residual.shape[1]
    half = features // 2
    core = lax.axis_index("core")
    ix, iy = lax.axis_index("x"), lax.axis_index("y")
    live_mask = jnp.arange(capacity) < counts[0]
    swap = [(0, 1), (1, 0)]

    mine = lax.dynamic_slice_in_dim(cotangent, core * half, half, axis=1)
    weight_t = out_weight.T
    mine, weight_t = lax.optimization_barrier((mine, weight_t))
    returned = lax.all_to_all(mine, ("x", "y", "z"), split_axis=0, concat_axis=0, tiled=True)
    block = spread(weight_t, "z").reshape(128, 1024)
    context_before = lax.ppermute(context, "x", RIGHT)
    context_after = lax.ppermute(context, "x", LEFT)
    block, context_before, context_after = lax.optimization_barrier(
        (block, context_before, context_after)
    )
    mid = capacity // 2
    context_top = lax.ppermute(context_before[:mid], "x", RIGHT)
    context_bottom = lax.ppermute(context_after[mid:], "x", LEFT)
    context_pieces = (context, context_after, context_top, context_bottom, context_before)
    a_block = jnp.concatenate(ring_gather(block[:, :512], "y")).reshape(4, 128, 512)
    b_block = jnp.concatenate(ring_gather(block[:, 512:], "x")).reshape(4, 128, 512)
    a_before = lax.ppermute(a_block, "x", RIGHT)
    a_after = lax.ppermute(a_block, "x", LEFT)
    b_before = lax.ppermute(b_block, "y", RIGHT)
    b_after = lax.ppermute(b_block, "y", LEFT)
    a_before, a_after, b_before, b_after, context_pieces = lax.optimization_barrier(
        (a_before, a_after, b_before, b_after, context_pieces)
    )
    a_top = lax.ppermute(a_before[:2], "x", RIGHT)
    a_bottom = lax.ppermute(a_after[2:], "x", LEFT)
    b_top = lax.ppermute(b_before[:2], "y", RIGHT)
    b_bottom = lax.ppermute(b_after[2:], "y", LEFT)
    pieces = (a_block, a_after, a_top, a_bottom, a_before)
    pieces = pieces + (b_block, b_after, b_top, b_bottom, b_before)
    pieces, returned = lax.optimization_barrier((pieces, returned))

    weight_t, partial_proj = project(context, pieces)
    weight_t = weight_t.reshape(2048, 1024)
    picked = returned.at[slot_codes].get(mode="promise_in_bounds")
    picked = jnp.where(live_mask[:, None], picked, jnp.zeros((), picked.dtype))
    other = lax.ppermute(picked, "core", swap)
    grad_out = jnp.where(
        core == 0,
        jnp.concatenate([picked, other], axis=1),
        jnp.concatenate([other, picked], axis=1),
    )
    projected = partial_proj + lax.ppermute(partial_proj, "core", swap)
    grad_resid = norm_back(projected, residual, bias_out, norm_gain, grad_out)

    def columns_of(step):
        at = lax.rem(ix + step, 4)
        return lax.dynamic_slice_in_dim(grad_resid, at * 512, 512, axis=1)

    def product(columns, rows):
        return lax.dot_general(
            columns, rows, (((0,), (0,)), ((), ())), preferred_element_type=F32
        )

    def half_of(step):
        at = lax.rem(ix + step, 4)
        return lax.dynamic_slice(grad_resid, (core * mid, at * 512), (mid, 512))

    fetched = jnp.concatenate([
        lax.ppermute(half_of(3), "x", LEFT),
        lax.ppermute(half_of(2), "x", ACROSS),
        lax.ppermute(half_of(1), "x", RIGHT),
    ])
    swapped = lax.ppermute(fetched, "core", swap)
    far_rows = jnp.concatenate(context_pieces[2:4])
    three = (context_pieces[1], far_rows, context_pieces[4])

    def halves(which):
        return jnp.concatenate(
            [lax.dynamic_slice_in_dim(rows, which * mid, mid, axis=0) for rows in three]
        )

    share = product(columns_of(0), context)
    share = share + product(fetched, halves(core))
    share = share + product(swapped, halves(1 - core))

    def strip_of(step):
        return lax.dynamic_slice_in_dim(share, lax.rem(iy + step, 4) * 128, 128, axis=0)

    total = collect(ring_reduce(strip_of, "y"), "z")
    replicas = lax.axis_size("x") * lax.axis_size("y") * lax.axis_size("z")
    grad_wout = (total / replicas).T
    grad_ctx = jnp.dot(grad_resid, weight_t, preferred_element_type=F32).astype(BF16)
    return (grad_resid, grad_ctx, grad_wout)


def solution(mesh):
    torus = Mesh(mesh.devices.reshape(4, 4, 8, 2), ("x", "y", "z", "core"))
    dp = ("x", "y", "z")
    return jax.shard_map(
        shards,
        mesh=torus,
        in_specs=(
            P(dp, "core"),
            P(dp, None),
            P(),
            P(),
            P("core", dp),
            P(dp, None),
            P(dp),
            P(dp),
        ),
        out_specs=(P(dp, None), P(dp, "core"), P("core", dp)),
        check_vma=False,
    )
```

```python
import jax
import jax.numpy as jnp
from jax import lax
from jax.experimental import pallas as pl
from jax.experimental.pallas import tpu as pltpu
from jax.sharding import Mesh, PartitionSpec as P

F32 = jnp.float32
BF16 = jnp.bfloat16
RIGHT = [(i, (i + 1) % 4) for i in range(4)]
LEFT = [(i, (i - 1) % 4) for i in range(4)]
ACROSS = [(i, (i + 2) % 4) for i in range(4)]


def norm_back(projected, residual, bias_out, norm_gain, grad_out):
    summed_in = residual.astype(F32) + projected + bias_out
    mean_in = jnp.mean(summed_in, axis=-1, keepdims=True)
    centred = summed_in - mean_in
    variance = jnp.mean(centred * centred, axis=-1, keepdims=True)
    inv_std = lax.rsqrt(variance + 1e-05)
    normed = centred * inv_std
    grad_norm = grad_out.astype(F32) * norm_gain
    first_mean = jnp.mean(grad_norm, axis=-1, keepdims=True)
    second_mean = jnp.mean(grad_norm * normed, axis=-1, keepdims=True)
    return (inv_std * (grad_norm - first_mean - normed * second_mean)).astype(BF16)


def ring_gather(piece, axis):
    mid = piece.shape[0] // 2
    before = lax.ppermute(piece, axis, RIGHT)
    after = lax.ppermute(piece, axis, LEFT)
    top = lax.ppermute(before[:mid], axis, RIGHT)
    bottom = lax.ppermute(after[mid:], axis, LEFT)
    return piece, after, top, bottom, before


def ring_reduce(chunk_of, axis):
    far = lax.ppermute(chunk_of(2).astype(BF16), axis, ACROSS)
    from_before = lax.ppermute(chunk_of(1).astype(BF16), axis, RIGHT)
    from_after = lax.ppermute(chunk_of(3).astype(BF16), axis, LEFT)
    return chunk_of(0) + from_before.astype(F32) + far.astype(F32) + from_after.astype(F32)


def project_kernel(*refs):
    context_ref, pieces = refs[0], refs[1:6]
    weight_ref, out_ref = refs[6], refs[7]
    placed, sems = refs[8], refs[9]
    ix, iy = lax.axis_index("x"), lax.axis_index("y")
    for ref, step, low in zip(pieces, (0, 1, 2, 2, 3), (0, 0, 0, 2, 0)):
        at = lax.rem(iy + step, 4)
        for k in range(ref.shape[0]):
            placed[lax.rem(ix + low + k, 4), at] = ref[k]
    copies = [
        pltpu.make_async_copy(placed.at[x], weight_ref.at[x], sems.at[x]) for x in range(4)
    ]
    for copy in copies:
        copy.start()
    for x in range(4):
        block = placed[x].reshape(512, 1024)
        out_ref[:, x * 512:(x + 1) * 512] = lax.dot_general(
            context_ref[...], block, (((1,), (1,)), ((), ())), preferred_element_type=F32
        )
    for copy in copies:
        copy.wait()


def project(context, pieces):
    rows = context.shape[0]
    vmem = pl.BlockSpec(memory_space=pltpu.VMEM)
    return pl.pallas_call(
        project_kernel,
        out_shape=(
            jax.ShapeDtypeStruct((4, 4, 128, 1024), BF16),
            jax.ShapeDtypeStruct((rows, 2048), F32),
        ),
        in_specs=[vmem] * 6,
        out_specs=(pl.BlockSpec(memory_space=pltpu.HBM), vmem),
        scratch_shapes=[
            pltpu.VMEM((4, 4, 128, 1024), BF16),
            pltpu.SemaphoreType.DMA((4,)),
        ],
        compiler_params=pltpu.CompilerParams(vmem_limit_bytes=40 << 20),
        cost_estimate=pl.CostEstimate(
            flops=2 * rows * 1024 * 2048, bytes_accessed=16 << 20, transcendentals=0
        ),
        name="project",
    )(context, *pieces)


def spread(piece, axis):
    ways = lax.axis_size(axis)
    whole = jnp.broadcast_to(piece[None], (ways,) + piece.shape)
    return lax.all_to_all(whole, axis, split_axis=0, concat_axis=0)


def collect(total, axis):
    ways = lax.axis_size(axis)
    share = total.astype(BF16).reshape(ways, -1, total.shape[1])
    got = lax.all_to_all(share, axis, split_axis=0, concat_axis=0)
    return jnp.sum(got.astype(F32), axis=0)


def shards(context, residual, bias_out, norm_gain, out_weight, cotangent, counts, slot_codes):
    capacity = slot_codes.shape[0]
    features = residual.shape[1]
    half = features // 2
    core = lax.axis_index("core")
    ix, iy = lax.axis_index("x"), lax.axis_index("y")
    live_mask = jnp.arange(capacity) < counts[0]
    swap = [(0, 1), (1, 0)]

    mine = lax.dynamic_slice_in_dim(cotangent, core * half, half, axis=1)
    weight_t = out_weight.T
    mine, weight_t = lax.optimization_barrier((mine, weight_t))
    returned = lax.all_to_all(mine, ("x", "y", "z"), split_axis=0, concat_axis=0, tiled=True)
    block = spread(weight_t, "z").reshape(128, 1024)
    context_before = lax.ppermute(context, "x", RIGHT)
    context_after = lax.ppermute(context, "x", LEFT)
    block, context_before, context_after = lax.optimization_barrier(
        (block, context_before, context_after)
    )
    mid = capacity // 2
    context_top = lax.ppermute(context_before[:mid], "x", RIGHT)
    context_bottom = lax.ppermute(context_after[mid:], "x", LEFT)
    context_pieces = (context, context_after, context_top, context_bottom, context_before)
    block = jnp.concatenate(ring_gather(block, "x")).reshape(4, 128, 1024)
    before = lax.ppermute(block, "y", RIGHT)
    after = lax.ppermute(block, "y", LEFT)
    before, after, context_pieces = lax.optimization_barrier((before, after, context_pieces))
    top = lax.ppermute(before[:2], "y", RIGHT)
    bottom = lax.ppermute(after[2:], "y", LEFT)
    pieces = (block, after, top, bottom, before)
    pieces, returned = lax.optimization_barrier((pieces, returned))

    weight_t, partial_proj = project(context, pieces)
    weight_t = weight_t.reshape(2048, 1024)
    picked = returned.at[slot_codes].get(mode="promise_in_bounds")
    picked = jnp.where(live_mask[:, None], picked, jnp.zeros((), picked.dtype))
    other = lax.ppermute(picked, "core", swap)
    grad_out = jnp.where(
        core == 0,
        jnp.concatenate([picked, other], axis=1),
        jnp.concatenate([other, picked], axis=1),
    )
    projected = partial_proj + lax.ppermute(partial_proj, "core", swap)
    grad_resid = norm_back(projected, residual, bias_out, norm_gain, grad_out)

    def columns_of(step):
        at = lax.rem(ix + step, 4)
        return lax.dynamic_slice_in_dim(grad_resid, at * 512, 512, axis=1)

    def product(columns, rows):
        return lax.dot_general(
            columns, rows, (((0,), (0,)), ((), ())), preferred_element_type=F32
        )

    def half_of(step):
        at = lax.rem(ix + step, 4)
        return lax.dynamic_slice(grad_resid, (core * mid, at * 512), (mid, 512))

    fetched = jnp.concatenate([
        lax.ppermute(half_of(3), "x", LEFT),
        lax.ppermute(half_of(2), "x", ACROSS),
        lax.ppermute(half_of(1), "x", RIGHT),
    ])
    swapped = lax.ppermute(fetched, "core", swap)
    far_rows = jnp.concatenate(context_pieces[2:4])
    three = (context_pieces[1], far_rows, context_pieces[4])

    def halves(which):
        return jnp.concatenate(
            [lax.dynamic_slice_in_dim(rows, which * mid, mid, axis=0) for rows in three]
        )

    share = product(columns_of(0), context)
    share = share + product(fetched, halves(core))
    share = share + product(swapped, halves(1 - core))

    def strip_of(step):
        return lax.dynamic_slice_in_dim(share, lax.rem(iy + step, 4) * 128, 128, axis=0)

    total = collect(ring_reduce(strip_of, "y"), "z")
    replicas = lax.axis_size("x") * lax.axis_size("y") * lax.axis_size("z")
    grad_wout = (total / replicas).T
    grad_ctx = jnp.dot(grad_resid, weight_t, preferred_element_type=F32).astype(BF16)
    return (grad_resid, grad_ctx, grad_wout)


def solution(mesh):
    torus = Mesh(mesh.devices.reshape(4, 4, 8, 2), ("x", "y", "z", "core"))
    dp = ("x", "y", "z")
    return jax.shard_map(
        shards,
        mesh=torus,
        in_specs=(
            P(dp, "core"),
            P(dp, None),
            P(),
            P(),
            P("core", dp),
            P(dp, None),
            P(dp),
            P(dp),
        ),
        out_specs=(P(dp, None), P(dp, "core"), P("core", dp)),
        check_vma=False,
    )
```
